32 devices in a mesh: fsdp: 16 (over z, y, x), head: 2 (over core).
Axes of the slice: x: 2, y: 2, z: 4, core: 2. Of those that a mesh axis runs over, the one named last changes fastest.
Arguments:
- tokens: bfloat16 [8192, 2048], P('fsdp'), may hold values from -6 to 6
- norm_gains: float32 [1, 2, 2048], replicated, may hold values from 0.1 to 1.9
- w_mixer: bfloat16 [1, 2048, 8, 1536], P(None, 'fsdp', 'head'), may hold values from -0.125 to 0.125
- w_out: bfloat16 [1, 4096, 2048], P(None, 'head', 'fsdp'), may hold values from -0.1875 to 0.1875
- w_up: bfloat16 [1, 2048, 4096], P(None, 'fsdp', 'head'), may hold values from -0.125 to 0.125
- w_down: bfloat16 [1, 4096, 2048], P(None, 'head', 'fsdp'), may hold values from -0.125 to 0.125
- seg_ids: int32 [8192], P('fsdp'), may hold values from 0 to 5, never falling along the last dimension, each value on 1 to 2048 neighbouring positions
- cotangent: bfloat16 [8192, 2048], P('fsdp'), may hold values from -6 to 6
Outputs:
- output: bfloat16 [8192, 2048], P('fsdp')
- input_grad: bfloat16 [8192, 2048], P('fsdp')
- gain_grad: float32 [1, 2, 2048], replicated
- mixer_grad: float32 [1, 2048, 8, 1536], P(None, 'fsdp', 'head')
- out_grad: float32 [1, 4096, 2048], P(None, 'head', 'fsdp')
- up_grad: float32 [1, 2048, 4096], P(None, 'fsdp', 'head')
- down_grad: float32 [1, 4096, 2048], P(None, 'head', 'fsdp')
The draws below stay inside these ranges and needn't reach their ends.
Inputs may be any that keep to these rules, and one draw needn't show every extreme that they name: `seg_ids`: sequence numbers never fall along the tokens; each sequence has 1 to 2048 tokens and one has exactly 2048.
All inputs are finite; a program needn't handle non-finite values.
Results may differ from the reference program's by a relative error of at most 0.02.
Values may be sent and summed in bfloat16 or wider, within the bound.
No kernel may reach another device: no remote copies, remote signals or barrier semaphores. Data moves between devices by JAX's collectives and lax.ppermute only.
A program may use at most 256 MiB of HBM per device.

```python
import math
import jax
import jax.numpy as jnp
import numpy as np
from jax import lax

D = 2048
HEADS = 8
KEY = 256
VALUE = 512
FF = 4096
LAYERS = 1
SEQ_MOST = 2048
TOK_DEV = 512
WIDTH = 1536
TOKENS = 8192
SEQS = 6
N_FSDP = 16


def level_of(rng, extent, cuts, smallest, largest):
    def one(dim, shards_of):
        heights = jax.random.uniform(jax.random.fold_in(jax.random.fold_in(rng, 6), dim), (shards_of,), jnp.float32, smallest / len(cuts), largest / len(cuts))
        return jnp.repeat(jnp.exp(heights), extent[dim] // shards_of).reshape((-1,) + (1,) * (len(extent) - dim - 1))

    loudness = one(*cuts[0])
    for cut in cuts[1:]:
        loudness = loudness * one(*cut)
    return loudness


def profile(number_of, total, most, slope):
    weights = [(1 << 20) // math.isqrt(rank ** slope) + 1 for rank in range(2, number_of + 1)]
    spare, counts = total - most - (number_of - 1), [1] * (number_of - 1)
    while spare > 0:
        free = [i for i in range(number_of - 1) if counts[i] < most]
        pool, budget = sum([weights[i] for i in free]), spare
        for i in free:
            extra = min(most - counts[i], max(1, budget * weights[i] // pool), spare)
            counts[i] = counts[i] + extra
            spare = spare - extra
    return np.array([most] + counts)


def ragged(rng, count, total, reach, slope):
    if count == 2:
        one = jax.random.randint(rng, (), max(1, total - reach), min(reach, total - 1) + 1)
        return jnp.stack([one, total - one])
    lengths = jnp.asarray(profile(count, total, reach, slope), jnp.int32)
    couples = (count - 1) // 2
    giver, receiver = lengths[1:1 + 2 * couples:2], lengths[2:2 + 2 * couples:2]
    slack = jnp.minimum(giver - 1, reach - receiver)
    shifted = jax.random.randint(jax.random.fold_in(rng, 1), (couples,), 0, 1 << 20) % (slack + 1)
    lengths = lengths.at[1:1 + 2 * couples:2].set(giver - shifted).at[2:2 + 2 * couples:2].set(receiver + shifted)
    return lengths[jax.random.permutation(jax.random.fold_in(rng, 2), count)]


def scatter_about(rng, shape, spread, reach, split=(), held_as=jnp.bfloat16):
    level = level_of(rng, shape, split, -0.22, 0.18) if split else 1.0
    entries = jax.random.normal(rng, shape, jnp.float32) * spread * level
    return jnp.minimum(jnp.maximum(entries, -reach), reach).astype(held_as)


def setup_inputs(seed: int = 0) -> dict:
    seeds = jax.random.split(jax.random.key(seed), 9)
    tokens = scatter_about(seeds[0], (TOKENS, D), 1.0, 6.0, ((0, 16),))
    norm_gains = jnp.clip(1.0 + 0.18 * jax.random.normal(seeds[1], (LAYERS, 2, D), jnp.float32), 0.1, 1.9)
    w_mixer = scatter_about(seeds[2], (LAYERS, D, HEADS, WIDTH), D ** -0.5, 0.125, ((1, 16), (2, 2)))
    w_out = scatter_about(seeds[3], (LAYERS, HEADS * VALUE, D), (HEADS * VALUE // 4) ** -0.5, 0.1875, ((1, 2), (2, 16)))
    w_up = scatter_about(seeds[4], (LAYERS, D, FF), D ** -0.5, 0.125, ((1, 16), (2, 2)))
    w_down = scatter_about(seeds[5], (LAYERS, FF, D), (FF // 2) ** -0.5, 0.125, ((1, 2), (2, 16)))
    seg_ids = jnp.searchsorted(jnp.cumsum(ragged(seeds[6], SEQS, TOKENS, SEQ_MOST, 1)), jnp.arange(TOKENS), side="right").astype(jnp.int32)
    cotangent = scatter_about(seeds[7], (TOKENS, D), 1.0, 6.0, ((0, 16),))
    return dict(tokens=tokens, norm_gains=norm_gains, w_mixer=w_mixer, w_out=w_out, w_up=w_up, w_down=w_down, seg_ids=seg_ids, cotangent=cotangent)


@jax.custom_vjp
def low(v):
    return lax.optimization_barrier(v.astype(jnp.bfloat16)).astype(jnp.float32)

@jax.custom_vjp
def low_back(v):
    return v

def low_keep(v):
    return (low(v), None)

def low_pass(kept, grad):
    return (grad,)

def back_keep(v):
    return (v, None)

def back_low(kept, grad):
    return (low(grad),)
low.defvjp(low_keep, low_pass)
low_back.defvjp(back_keep, back_low)
highest_precision = lax.Precision.HIGHEST
eps_norm = 1e-05
eps_group = 1e-06

def matmul(left, right):
    return jnp.dot(left, right, precision=highest_precision)

def layer_norm(stream, gain):
    centered = stream - lax.optimization_barrier(jnp.mean(stream, axis=-1, keepdims=True))
    scaled = lax.rsqrt(lax.optimization_barrier(jnp.mean(centered * centered, axis=-1, keepdims=True)) + eps_norm)
    return centered * scaled * gain

def retain_block(carry, inputs):
    state_carry, last_id = carry
    query_rows, key_matrix_rows, value_rows, segment = inputs
    log_rates = jnp.log1p(-jnp.exp2(-5.0 - jnp.arange(HEADS, dtype=jnp.float32)))
    length = segment.shape[0]
    places = jnp.arange(length)
    first_id = segment[0]
    final_id = segment[length - 1]
    joined = (last_id == first_id).astype(jnp.float32)
    offset = places[:, None] - places[None, :]
    valid = (offset >= 0) & (segment[:, None] == segment[None, :])
    decay = jnp.where(valid[None], jnp.exp(jnp.maximum(offset, 0).astype(jnp.float32)[None] * log_rates[:, None, None]), 0.0)
    scores = low_back(jnp.einsum('nhk,mhk->hnm', query_rows, key_matrix_rows, precision=highest_precision))
    weights = low(scores * decay)
    intra = jnp.einsum('hnm,mhv->nhv', weights, value_rows, precision=highest_precision)
    leading_weight = joined * (segment == first_id).astype(jnp.float32)[:, None] * jnp.exp((places[:, None] + 1).astype(jnp.float32) * log_rates[None, :])
    cross_segment = leading_weight[:, :, None] * jnp.einsum('baf,afu->bau', query_rows, state_carry, precision=highest_precision)
    trailing_weight = (segment == final_id).astype(jnp.float32)[:, None] * jnp.exp((length - 1 - places)[:, None].astype(jnp.float32) * log_rates[None, :])
    local_part = jnp.einsum('fdg,fde->dge', key_matrix_rows * trailing_weight[:, :, None], value_rows, precision=highest_precision)
    carry_on = joined * (first_id == final_id).astype(jnp.float32) * jnp.exp(length * log_rates)
    new_state = local_part + carry_on[:, None, None] * state_carry
    return ((new_state, final_id), intra + cross_segment)

def retention(query_rows, key_matrix_rows, value_rows, seg_ids):
    blocks = N_FSDP
    inputs = (query_rows.reshape(blocks, TOK_DEV, HEADS, KEY), key_matrix_rows.reshape(blocks, TOK_DEV, HEADS, KEY), value_rows.reshape(blocks, TOK_DEV, HEADS, VALUE), seg_ids.reshape(blocks, TOK_DEV))
    start = (jnp.zeros((HEADS, KEY, VALUE), jnp.float32), jnp.int32(-1))
    unused, mixed = lax.scan(jax.checkpoint(retain_block), start, inputs)
    return mixed.reshape(blocks * TOK_DEV, HEADS, VALUE)

def reference(tokens, norm_gains, w_mixer, w_out, w_up, w_down, seg_ids, cotangent):

    def forward(stream, gains, mixer, out_w, up_w, down_w):
        for depth in range(LAYERS):
            hidden = low(layer_norm(stream, gains[depth, 0]))
            projected = matmul(hidden, mixer[depth].reshape(D, HEADS * WIDTH)).reshape(-1, HEADS, WIDTH)
            query_rows = low(low_back(projected[:, :, :KEY]))
            key_matrix_rows = low(low_back(projected[:, :, KEY:2 * KEY]))
            value_rows = low(low_back(projected[:, :, 2 * KEY:2 * KEY + VALUE]))
            gate_raw = low_back(projected[:, :, 2 * KEY + VALUE:])
            mixed = low_back(retention(query_rows, key_matrix_rows, value_rows, seg_ids))
            normed = mixed * lax.rsqrt(lax.optimization_barrier(jnp.mean(mixed * mixed, axis=-1, keepdims=True)) + eps_group)
            gated = low((jax.nn.silu(gate_raw) * normed).reshape(-1, HEADS * VALUE))
            stream = stream + low_back(matmul(gated, out_w[depth]))
            hidden2 = low(layer_norm(stream, gains[depth, 1]))
            act = low(jax.nn.gelu(low_back(matmul(hidden2, up_w[depth])), approximate=False))
            stream = stream + low_back(matmul(act, down_w[depth]))
        return stream
    floats = (tokens.astype(jnp.float32), norm_gains.astype(jnp.float32), w_mixer.astype(jnp.float32), w_out.astype(jnp.float32), w_up.astype(jnp.float32), w_down.astype(jnp.float32))
    result, pull = jax.vjp(forward, *floats)
    grads = pull(cotangent.astype(jnp.float32))
    return (result.astype(jnp.bfloat16), grads[0].astype(jnp.bfloat16), grads[1], grads[2], grads[3], grads[4], grads[5])
```

```python
from functools import partial

import jax
import jax.numpy as jnp
from jax import lax
from jax.experimental import pallas as pl
from jax.experimental.pallas import tpu as pltpu
from jax.sharding import Mesh, PartitionSpec as P

HEADS = 8
KEY = 256
VALUE = 512
SEQ_MOST = 2048

eps_norm = 1e-05
eps_group = 1e-06
bf16 = jnp.bfloat16
f32 = jnp.float32


def team_size(devices, heads_here):
    team = 4
    while heads_here % team or devices % team:
        team //= 2
    return team


def dot(a, b, left=1, right=0):
    return lax.dot_general(a, b, (((left,), (right,)), ((), ())), preferred_element_type=f32)


def bdot(a, b, left, right):
    return lax.dot_general(
        a, b, (((left,), (right,)), ((0,), (0,))), preferred_element_type=f32
    )


def layer_norm(stream, gain):
    centered = stream - jnp.mean(stream, axis=-1, keepdims=True)
    scaled = lax.rsqrt(jnp.mean(centered * centered, axis=-1, keepdims=True) + eps_norm)
    normed = centered * scaled
    return (normed * gain, normed, scaled)


def norm_back(grad_out, normed, scaled, gain):
    grad_norm = grad_out * gain
    inner = jnp.mean(grad_norm, axis=-1, keepdims=True)
    along = jnp.mean(grad_norm * normed, axis=-1, keepdims=True)
    return (scaled * (grad_norm - inner - normed * along), jnp.sum(grad_out * normed, axis=0))


def swap(value, axis, d):
    count = lax.axis_size(axis)
    return lax.ppermute(value, axis, [(i, i ^ d) for i in range(count)])


def shift(value, steps):
    count = lax.axis_size("group")
    pairs = [(i, i + steps) for i in range(count) if 0 <= i + steps < count]
    return lax.ppermute(value, "group", pairs)


def total(value):
    for axis in ("head", "team", "group"):
        step = 1
        while step < lax.axis_size(axis):
            value = value + swap(value, axis, step)
            step *= 2
    return value


def straight(pieces, axis):
    mine = lax.axis_index(axis)
    pieces = list(pieces)
    bit = 1
    while bit < len(pieces):
        odd = (mine & bit) != 0
        pieces = [jnp.where(odd, pieces[i ^ bit], pieces[i]) for i in range(len(pieces))]
        bit *= 2
    return pieces


def deal(pick):
    mine = lax.axis_index("team")
    got = [pick(mine)]
    for d in range(1, lax.axis_size("team")):
        got.append(swap(pick(mine ^ d), "team", d))
    return straight(got, "team")


def join(parts):
    rows = parts[0].shape[0]
    out = jnp.zeros((rows * len(parts),) + parts[0].shape[1:], parts[0].dtype)
    for i, part in enumerate(parts):
        out = lax.dynamic_update_slice_in_dim(out, part, i * rows, 0)
    return out


def share(own):
    rows = join([own] + [swap(own, "team", d) for d in range(1, lax.axis_size("team"))])
    return [rows] + [swap(rows, "head", e) for e in range(1, lax.axis_size("head"))]


def after(values, first):
    return lax.optimization_barrier((values, first))[0]


def reduce(rows, weight, right):
    team = lax.axis_size("team")
    piece = rows[0].shape[0] // team
    other = [
        swap(dot(rows[e], weight, 1, right).astype(bf16), "head", e) for e in range(1, len(rows))
    ]

    def part(d):
        here = slice(d * piece, (d + 1) * piece)
        value = dot(rows[0][here], weight, 1, right)
        for got in other:
            value = value + got[here].astype(f32)
        return value

    sent = [part(d).astype(bf16) for d in range(1, team)]
    got = [swap(v, "team", d) for d, v in enumerate(sent, 1)]
    value = part(0)
    for v in got:
        value = value + v.astype(f32)
    return value, sent


def grads(left, right):
    value = dot(left[0], right[0], 0, 0)
    for a, b in zip(left[1:], right[1:]):
        value = value + dot(a, b, 0, 0)
    return lax.psum_scatter(value.astype(bf16), "group", scatter_dimension=0, tiled=True)


def chosen(refs, at):
    team = at[1]
    value = refs[0][...]
    for e in range(1, len(refs)):
        value = jnp.where(at[0] >= e * team, refs[e][...], value)
    return value


def weights_of(rate, seg_col, seg_row):
    size = seg_col.shape[0]
    row = lax.broadcasted_iota(jnp.int32, (size, size), 0)
    col = lax.broadcasted_iota(jnp.int32, (size, size), 1)
    offset = row - col
    valid = (offset >= 0) & (seg_col == seg_row)
    decay = jnp.where(valid, jnp.exp(jnp.maximum(offset, 0).astype(f32) * rate), 0.0)
    place = lax.broadcasted_iota(jnp.int32, (size, 1), 0)
    ahead = jnp.exp((place + 1).astype(f32) * rate)
    behind = jnp.exp((size - 1 - place).astype(f32) * rate)
    return decay, ahead, behind


def forward_kernel(cores, team, order, firsts, lasts, before_group, floats, *refs):
    qkv_refs = refs[:cores]
    col_ref, row_ref, start_ref, normed_ref, scale_ref, states_ref, state = refs[cores:]
    step = pl.program_id(0)
    rank = step
    at = order[rank]
    rate = floats[0]

    @pl.when(step == 0)
    def _():
        state[...] = start_ref[...].astype(f32)

    qkv = chosen(qkv_refs, (at, team))
    query, key, value = qkv[:, :KEY], qkv[:, KEY : 2 * KEY], qkv[:, 2 * KEY :]
    seg = col_ref[...]
    grown = jnp.exp(jnp.full((1, 1), 1.0, f32) * floats[1])
    decay, ahead, behind = weights_of(rate, seg, row_ref[0])
    first, last = firsts[at], lasts[at]
    before = jnp.where(rank == 0, before_group[0], lasts[order[jnp.maximum(rank - 1, 0)]])
    ahead = jnp.where((seg == first) & (before == first), ahead, 0.0)
    behind = jnp.where(seg == last, behind, 0.0)
    carry = jnp.where((before == first) & (first == last), grown, 0.0)
    held = state[...].astype(bf16)
    states_ref[0] = held
    scores = dot(query, key, 1, 1)
    weights = (scores * decay).astype(bf16)
    mixed = dot(weights, value) + ahead * dot(query, held)
    scale = lax.rsqrt(jnp.mean(mixed * mixed, axis=-1, keepdims=True) + eps_group)
    normed_ref[...] = mixed * scale
    scale_ref[...] = scale
    state[...] = dot((key * behind).astype(bf16), value, 0, 0) + carry * state[...]


def backward_kernel(cores, team, order, firsts, lasts, before_group, floats, *refs):
    groups = [refs[i * cores : (i + 1) * cores] for i in range(4)]
    qkv_refs, mixed_refs, rest_refs, gate_refs = groups
    states_ref, col_ref, row_ref, start_ref, out_ref, state = refs[4 * cores :]
    step = pl.program_id(0)
    rank = pl.num_programs(0) - 1 - step
    at = order[rank]
    rate = floats[0]

    @pl.when(step == 0)
    def _():
        state[...] = start_ref[...].astype(f32)

    qkv = chosen(qkv_refs, (at, team))
    grad = chosen(mixed_refs, (at, team))
    query, key, value = qkv[:, :KEY], qkv[:, KEY : 2 * KEY], qkv[:, 2 * KEY :]
    seg = col_ref[...]
    grown = jnp.exp(jnp.full((1, 1), 1.0, f32) * floats[1])
    decay, ahead, behind = weights_of(rate, seg, row_ref[0])
    first, last = firsts[at], lasts[at]
    before = jnp.where(rank == 0, before_group[0], lasts[order[jnp.maximum(rank - 1, 0)]])
    ahead = jnp.where((seg == first) & (before == first), ahead, 0.0)
    behind = jnp.where(seg == last, behind, 0.0)
    carry = jnp.where((before == first) & (first == last), grown, 0.0)
    held = state[...].astype(bf16)
    weights = (dot(query, key, 1, 1) * decay).astype(bf16)
    grad_rest = chosen(rest_refs, (at, team))
    grad_weights = dot(grad, value, 1, 1) + dot(grad_rest, value, 1, 1)
    grad_scores = (grad_weights * decay).astype(bf16)
    grad_query = dot(grad_scores, key) + ahead * dot(grad, states_ref[0], 1, 1)
    grad_key = dot(grad_scores, query, 0, 0) + behind * dot(value, held, 1, 1)
    grad_value = dot(weights, grad, 0, 0) + behind * dot(key, held)
    out_ref[:, :KEY] = grad_query.astype(bf16)
    out_ref[:, KEY : 2 * KEY] = grad_key.astype(bf16)
    out_ref[:, 2 * KEY : 2 * KEY + VALUE] = grad_value.astype(bf16)
    out_ref[:, 2 * KEY + VALUE :] = chosen(gate_refs, (at, team))
    state[...] = dot((query * ahead).astype(bf16), grad, 0, 0) + carry * state[...]


def walk(kernel, cores, team, edges, split, whole, outs, reverse, flops, moved):
    chunks = cores * team

    def at(step, order):
        return order[chunks - 1 - step] if reverse else order[step]

    def block(e, width, size):
        return pl.BlockSpec(
            (size, width),
            lambda i, order, *_: (jnp.clip(at(i, order) - e * team, 0, team - 1), 0),
        )

    def spec(shape, each):
        zeros = (0,) * (len(shape) - 1)
        if each:
            return pl.BlockSpec(shape, lambda i, order, *_: (at(i, order),) + zeros)
        return pl.BlockSpec(shape, lambda i, order, *_: (0,) + zeros)

    arrays, specs = [], []
    for group in split:
        for e, array in enumerate(group):
            arrays.append(array)
            specs.append(block(e, array.shape[1], array.shape[0] // team))
    for array, shape, each in whole:
        arrays.append(array)
        specs.append(spec(shape, each))
    return pl.pallas_call(
        partial(kernel, cores, team),
        grid_spec=pltpu.PrefetchScalarGridSpec(
            num_scalar_prefetch=len(edges),
            grid=(chunks,),
            in_specs=specs,
            out_specs=[spec(shape, each) for _, shape, each in outs],
            scratch_shapes=[pltpu.VMEM((KEY, VALUE), f32)],
        ),
        out_shape=[shape for shape, _, _ in outs],
        compiler_params=pltpu.CompilerParams(dimension_semantics=("arbitrary",)),
        cost_estimate=pl.CostEstimate(flops=flops, bytes_accessed=moved, transcendentals=0),
    )(*edges, *arrays)


def gate_back_kernel(grad_ref, weight_ref, gate_ref, normed_ref, scale_ref, gate_out, mixed_out, rest_out):
    grad_gated = dot(grad_ref[...], weight_ref[...])
    gate = gate_ref[...]
    normed = normed_ref[...]
    sigmoid = 1.0 / (1.0 + jnp.exp(-gate))
    gate_out[...] = (
        grad_gated * normed * (sigmoid + gate * sigmoid * (1.0 - sigmoid))
    ).astype(bf16)
    grad_normed = grad_gated * (gate * sigmoid)
    along = jnp.mean(grad_normed * normed, axis=-1, keepdims=True)
    grad_mixed = scale_ref[...] * (grad_normed - normed * along)
    rounded = grad_mixed.astype(bf16)
    mixed_out[...] = rounded
    rest_out[...] = (grad_mixed - rounded.astype(f32)).astype(bf16)


def gate_back(grad, weight, gate, normed, scale, e):
    rows, width = grad.shape
    size = min(256, rows)
    steps = rows // size
    own = lambda i: (i, 0)
    far = lambda i: (e * steps + i, 0)
    shape = jax.ShapeDtypeStruct((rows, VALUE), bf16)
    return pl.pallas_call(
        gate_back_kernel,
        grid=(steps,),
        in_specs=[
            pl.BlockSpec((size, width), own),
            pl.BlockSpec(weight.shape, lambda i: (0, 0)),
            pl.BlockSpec((size, VALUE), own),
            pl.BlockSpec((size, VALUE), far),
            pl.BlockSpec((size, 1), far),
        ],
        out_specs=[pl.BlockSpec((size, VALUE), own)] * 3,
        out_shape=[shape] * 3,
        compiler_params=pltpu.CompilerParams(dimension_semantics=("arbitrary",)),
        cost_estimate=pl.CostEstimate(
            flops=2 * rows * width * VALUE, bytes_accessed=2 * rows * width, transcendentals=0
        ),
    )(grad, weight, gate, normed, scale)


def shards(tokens, norm_gains, w_mixer, w_out, w_up, w_down, seg_ids, cotangent):
    team, groups, cores = (lax.axis_size(a) for a in ("team", "group", "head"))
    g, j, c = (lax.axis_index(a) for a in ("group", "team", "head"))
    heads_here = w_mixer.shape[2]
    length, width = tokens.shape
    size = length // cores
    chunks = team
    near = range(cores)
    units = w_up.shape[2] // team

    rows_here = w_mixer.shape[1]
    mixer_slabs = w_mixer[0].transpose(1, 0, 2)
    rest = jnp.concatenate(
        [
            w_out[0].reshape(team, VALUE, rows_here).transpose(0, 2, 1),
            w_up[0].reshape(rows_here, team, units).transpose(1, 0, 2),
            w_down[0].reshape(team, units, rows_here).transpose(0, 2, 1),
        ],
        axis=2,
    )
    mixer_rows = join(deal(lambda m: lax.dynamic_index_in_dim(mixer_slabs, m, 0, keepdims=False)))
    whole = partial(lax.all_gather, axis_name="group", axis=0, tiled=True)
    w_qkv = whole(mixer_rows[:, : 2 * KEY + VALUE])
    w_gate = whole(mixer_rows[:, 2 * KEY + VALUE :])
    segs = [seg_ids] + [swap(seg_ids, "team", d) for d in range(1, team)]
    seg = jnp.stack(
        [
            lax.dynamic_slice_in_dim(segs[d], (c ^ e) * size, size, 0)
            for e in near
            for d in range(team)
        ]
    )
    chunks = cores * team
    rank = jnp.arange(chunks)
    order = (((rank % cores) ^ c) * team + ((rank // cores) ^ j)).astype(jnp.int32)
    place = jnp.stack([(j ^ d) * length + (c ^ e) * size for e in near for d in range(team)])
    group_length = team * length
    group_first = jnp.min(seg, keepdims=True)
    group_last = jnp.max(seg, keepdims=True)
    before_group = shift(group_last + 1, 1) - 1
    head = c * heads_here + j
    rate = jnp.log1p(-jnp.exp2(-5.0 - head.astype(f32)))
    floats = rate * jnp.array([1.0, size], f32)
    seg_col = seg.reshape(-1, 1)
    seg_row = seg[:, None, :]
    token = (place[:, None] + jnp.arange(size)).reshape(-1, 1)
    to_end = jnp.where(
        seg_col == group_last, jnp.exp((group_length - 1 - token).astype(f32) * rate), 0.0
    )
    from_start = jnp.where(
        seg_col == before_group, jnp.exp((token + 1).astype(f32) * rate), 0.0
    )
    through = jnp.where(
        (before_group == group_first) & (group_first == group_last),
        jnp.exp(group_length * rate),
        0.0,
    )
    edges = (order, seg[:, 0], seg[:, size - 1], before_group.reshape(1), floats)
    hops = -(-(SEQ_MOST - 1) // group_length)
    rows = team * size

    def here(value, e):
        return value[e * rows : (e + 1) * rows]

    def state_sum(left, factor, right):
        return sum(
            dot((left[e] * here(factor, e)).astype(bf16), right[e], 0, 0) for e in near
        )

    def passed(value, steps):
        state = shift(value.astype(bf16), steps)
        for _ in range(hops - 1):
            state = shift((value + through * state.astype(f32)).astype(bf16), steps)
        return state

    gain_one, gain_two = norm_gains[0, 0], norm_gains[0, 1]
    stream = lax.dynamic_slice_in_dim(tokens, c * size, size, 0).astype(f32)
    cot = lax.dynamic_slice_in_dim(cotangent, c * size, size, 0)
    hidden_own, normed1, scaled1 = layer_norm(stream, gain_one)
    hidden = share(after(hidden_own.astype(bf16), mixer_rows))
    rest = after(rest, hidden[0])
    rest_rows = join(deal(lambda m: lax.dynamic_index_in_dim(rest, m, 0, keepdims=False)))
    w_o = whole(rest_rows[:, :VALUE])
    w_u = whole(rest_rows[:, VALUE : VALUE + units])
    w_d = whole(rest_rows[:, VALUE + units :])
    cot_all = share(after(cot, rest_rows))
    hidden = after(hidden, cot_all[0])

    qkv = [dot(h, w_qkv).astype(bf16) for h in hidden]
    end_state = state_sum(
        [v[:, KEY : 2 * KEY] for v in qkv], to_end, [v[:, 2 * KEY :] for v in qkv]
    )
    chunk_flops = 2 * size * size * (KEY + VALUE) + 4 * size * KEY * VALUE
    normed, scale, states = walk(
        forward_kernel,
        cores,
        team,
        edges,
        [qkv],
        [
            (seg_col, (size, 1), True),
            (seg_row, (1, 1, size), True),
            (passed(end_state, 1), (KEY, VALUE), False),
        ],
        [
            (jax.ShapeDtypeStruct((chunks * size, VALUE), f32), (size, VALUE), True),
            (jax.ShapeDtypeStruct((chunks * size, 1), f32), (size, 1), True),
            (jax.ShapeDtypeStruct((chunks, KEY, VALUE), bf16), (1, KEY, VALUE), True),
        ],
        False,
        chunks * chunk_flops,
        chunks * size * 4096,
    )
    gate = [dot(h, w_gate) for h in hidden]
    gated = [
        (gate[e] * jax.nn.sigmoid(gate[e]) * here(normed, e)).astype(bf16)
        for e in near
    ]
    stream = stream + reduce(gated, w_o, 1)[0]

    hidden2_own, normed2, scaled2 = layer_norm(stream, gain_two)
    hidden2 = share(hidden2_own.astype(bf16))
    gelu = partial(jax.nn.gelu, approximate=False)
    acts = [jax.vjp(gelu, dot(h, w_u)) for h in hidden2]
    act = [a.astype(bf16) for a, _ in acts]

    def both_cores(rows):
        rows = rows.astype(bf16)
        got = [rows] + [swap(rows, "head", e) for e in range(1, cores)]
        return join(straight(got, "head"))

    grad_up = [
        pull(dot(t, w_d))[0].astype(bf16) for t, (_, pull) in zip(cot_all, acts)
    ]
    grad_hidden2, sent = reduce(grad_up, w_u, 1)
    down_done = grads(after(cot_all, sent), act)
    up_done = grads(after(hidden2, sent), grad_up)
    norm_part, gain_grad_two = norm_back(grad_hidden2, normed2, scaled2, gain_two)
    grad = cot.astype(f32) + norm_part
    grad_all = share(grad.astype(bf16))
    backs = [gate_back(grad_all[e], w_o, gate[e], normed, scale, e) for e in near]
    grad_gate, grad_mixed, mixed_rest = ([v[i] for v in backs] for i in range(3))
    gate_done = grads(hidden, grad_gate)
    stream = stream + reduce(after(act, grad_all[0]), w_d, 1)[0]
    output = both_cores(stream)
    grad_before = state_sum([v[:, :KEY] for v in qkv], from_start, grad_mixed)
    (proj,) = walk(
        backward_kernel,
        cores,
        team,
        edges,
        [qkv, grad_mixed, mixed_rest, grad_gate],
        [
            (states, (1, KEY, VALUE), True),
            (seg_col, (size, 1), True),
            (seg_row, (1, 1, size), True),
            (passed(grad_before, -1), (KEY, VALUE), False),
        ],
        [
            (
                jax.ShapeDtypeStruct((chunks * size, 2 * KEY + 2 * VALUE), bf16),
                (size, 2 * KEY + 2 * VALUE),
                True,
            ),
        ],
        True,
        3 * chunks * chunk_flops,
        chunks * size * 12000,
    )
    proj = after(proj, stream)
    grad_proj = [here(proj, e) for e in near]
    qkv_done = grads(hidden, [v[:, : 2 * KEY + VALUE] for v in grad_proj])
    out_done = grads(grad_all, gated)
    grad_hidden = reduce(grad_proj, jnp.concatenate([w_qkv, w_gate], axis=1), 1)[0]
    norm_part, gain_grad_one = norm_back(grad_hidden, normed1, scaled1, gain_one)
    input_grad = both_cores(grad + norm_part)
    gain_grad = total(jnp.stack([gain_grad_one, gain_grad_two]))

    def own_rows(done):
        return deal(lambda m: lax.dynamic_slice_in_dim(done, m * rows_here, rows_here, 0))

    def own_wide(done):
        return jnp.stack(own_rows(done), axis=1).astype(f32)

    mixer_grad = jnp.concatenate(
        [own_wide(v) for v in (qkv_done, gate_done)], axis=-1
    )
    up_grad = jnp.concatenate(own_rows(up_done), axis=1).astype(f32)
    out_grad = jnp.concatenate([v.T for v in own_rows(out_done)], axis=0).astype(f32)
    down_grad = jnp.concatenate([v.T for v in own_rows(down_done)], axis=0).astype(f32)
    return (
        output,
        input_grad,
        gain_grad[None],
        mixer_grad[None],
        out_grad[None],
        up_grad[None],
        down_grad[None],
    )


def solution(mesh):
    devices, cores = mesh.devices.shape
    team = team_size(devices, HEADS // cores)
    fine = Mesh(mesh.devices.reshape(devices // team, team, cores), ("group", "team", "head"))
    fsdp = ("group", "team")
    return jax.shard_map(
        shards,
        mesh=fine,
        in_specs=(
            P(fsdp, None),
            P(),
            P(None, fsdp, "head", None),
            P(None, "head", fsdp),
            P(None, fsdp, "head"),
            P(None, "head", fsdp),
            P(fsdp),
            P(fsdp, None),
        ),
        out_specs=(
            P(fsdp, None),
            P(fsdp, None),
            P(),
            P(None, fsdp, "head", None),
            P(None, "head", fsdp),
            P(None, fsdp, "head"),
            P(None, "head", fsdp),
        ),
        check_vma=False,
    )
```

```python
from functools import partial

import jax
import jax.numpy as jnp
from jax import lax
from jax.experimental import pallas as pl
from jax.experimental.pallas import tpu as pltpu
from jax.sharding import Mesh, PartitionSpec as P


HEADS = 8
KEY = 256
VALUE = 512
SEQ_MOST = 2048

eps_norm = 1e-05
eps_group = 1e-06
bf16 = jnp.bfloat16
f32 = jnp.float32


def team_size(devices, heads_here):
    team = 4
    while heads_here % team or devices % team:
        team //= 2
    return team


def dot(a, b, left=1, right=0):
    return lax.dot_general(a, b, (((left,), (right,)), ((), ())), preferred_element_type=f32)


def layer_norm(stream, gain):
    centered = stream - jnp.mean(stream, axis=-1, keepdims=True)
    scaled = lax.rsqrt(jnp.mean(centered * centered, axis=-1, keepdims=True) + eps_norm)
    normed = centered * scaled
    return (normed * gain, normed, scaled)


def norm_back(grad_out, normed, scaled, gain):
    grad_norm = grad_out * gain
    inner = jnp.mean(grad_norm, axis=-1, keepdims=True)
    along = jnp.mean(grad_norm * normed, axis=-1, keepdims=True)
    return (scaled * (grad_norm - inner - normed * along), jnp.sum(grad_out * normed, axis=0))


def swap(value, axis, d):
    count = lax.axis_size(axis)
    return lax.ppermute(value, axis, [(i, i ^ d) for i in range(count)])


def shift(value, steps):
    count = lax.axis_size("group")
    pairs = [(i, i + steps) for i in range(count) if 0 <= i + steps < count]
    return lax.ppermute(value, "group", pairs)


def total(value):
    for axis in ("head", "team", "group"):
        parts = [value] + [swap(value, axis, d) for d in range(1, lax.axis_size(axis))]
        while len(parts) > 1:
            parts = [parts[k] + parts[k + 1] for k in range(0, len(parts), 2)]
        value = parts[0]
    return value


def straight(pieces, axis):
    mine = lax.axis_index(axis)
    pieces = list(pieces)
    bit = 1
    while bit < len(pieces):
        odd = (mine & bit) != 0
        pieces = [jnp.where(odd, pieces[i ^ bit], pieces[i]) for i in range(len(pieces))]
        bit *= 2
    return pieces


def deal(pick):
    mine = lax.axis_index("team")
    got = [pick(mine)]
    for d in range(1, lax.axis_size("team")):
        got.append(swap(pick(mine ^ d), "team", d))
    return straight(got, "team")


def join(parts):
    rows = parts[0].shape[0]
    out = jnp.zeros((rows * len(parts),) + parts[0].shape[1:], parts[0].dtype)
    for i, part in enumerate(parts):
        out = lax.dynamic_update_slice_in_dim(out, part, i * rows, 0)
    return out


def share(own):
    parts = [own] + [swap(own, "team", d) for d in range(1, lax.axis_size("team"))]
    rows = join(parts)
    return [rows] + [swap(rows, "head", e) for e in range(1, lax.axis_size("head"))]


def after(values, first):
    return lax.optimization_barrier((values, first))[0]


def reduce_kernel(team, rows_ref, weight_ref, *refs):
    others, outs = refs[: len(refs) - team], refs[len(refs) - team :]
    total = dot(rows_ref[...], weight_ref[...], 1, 1)
    for other in others:
        total = total + other[...].astype(f32)
    piece = total.shape[0] // team
    for d, out in enumerate(outs):
        out[...] = total[d * piece : (d + 1) * piece].astype(out.dtype)


def reduce(rows, weight, column):
    team, cores = lax.axis_size("team"), len(rows)
    count, depth = rows[0].shape
    width = weight.shape[0]
    step = min(1024 if depth <= 512 else 512, width)
    part = weight[:, column * depth : (column + 1) * depth]
    first = [dot(rows[e], part, 1, 1).astype(bf16) for e in range(1, cores)]
    others = [swap(v, "head", e) for e, v in enumerate(first, 1)]
    piece = count // team
    out = pl.pallas_call(
        partial(reduce_kernel, team),
        grid=(width // step,),
        in_specs=[
            pl.BlockSpec((count, depth), lambda i: (0, 0)),
            pl.BlockSpec((step, depth), lambda i: (i, column)),
        ]
        + [pl.BlockSpec((count, step), lambda i: (0, i))] * (cores - 1),
        out_specs=[pl.BlockSpec((piece, step), lambda i: (0, i))] * team,
        out_shape=[jax.ShapeDtypeStruct((piece, width), bf16 if d else f32) for d in range(team)],
        compiler_params=pltpu.CompilerParams(dimension_semantics=("arbitrary",)),
        cost_estimate=pl.CostEstimate(
            flops=2 * count * depth * width,
            bytes_accessed=2 * width * (depth + 2 * count),
            transcendentals=0,
        ),
    )(rows[0], weight, *others)
    got = [swap(out[d], "team", d) for d in range(1, team)]
    value = out[0]
    for v in got:
        value = value + v.astype(f32)
    return value, out


def grads(left, right):
    value = dot(left[0], right[0], 0, 0)
    for a, b in zip(left[1:], right[1:]):
        value = value + dot(a, b, 0, 0)
    value = value.astype(bf16)
    return lax.psum_scatter(value, "group", scatter_dimension=0, tiled=True)


SUB = 128


def blocks_of(ref):
    size = min(SUB, ref.shape[0])
    return [slice(i, i + size) for i in range(0, ref.shape[0], size)]


def unit_kernel(hidden_ref, weight_ref, grad_ref, act_out, grad_out):
    for at in blocks_of(hidden_ref):
        value = dot(hidden_ref[at], weight_ref[...])
        cumulative = 0.5 + 0.5 * lax.erf(value * (0.5**0.5))
        density = jnp.exp(-0.5 * value * value) * 0.3989422804014327
        act_out[at] = (value * cumulative).astype(bf16)
        grad_out[at] = (grad_ref[at] * (cumulative + value * density)).astype(bf16)


def unit_step(hidden, weight, grad, units):
    rows, width = hidden.shape
    size = min(256, rows)
    own = lambda i: (i, 0)
    shape = jax.ShapeDtypeStruct((rows, units), bf16)
    return pl.pallas_call(
        unit_kernel,
        grid=(rows // size,),
        in_specs=[
            pl.BlockSpec((size, width), own),
            pl.BlockSpec((width, units), lambda i: (0, 0)),
            pl.BlockSpec((size, units), own),
        ],
        out_specs=[pl.BlockSpec((size, units), own)] * 2,
        out_shape=[shape] * 2,
        compiler_params=pltpu.CompilerParams(dimension_semantics=("arbitrary",)),
        cost_estimate=pl.CostEstimate(
            flops=2 * rows * width * units, bytes_accessed=2 * rows * width, transcendentals=0
        ),
    )(hidden, weight, grad)


def chosen(refs, at):
    team = at[1]
    value = refs[0][...]
    for e in range(1, len(refs)):
        value = jnp.where(at[0] >= e * team, refs[e][...], value)
    return value


def weights_of(rate, seg_col, seg_row):
    size = seg_col.shape[0]
    row = lax.broadcasted_iota(jnp.int32, (size, size), 0)
    col = lax.broadcasted_iota(jnp.int32, (size, size), 1)
    offset = row - col
    valid = (offset >= 0) & (seg_col == seg_row)
    decay = jnp.where(valid, jnp.exp(jnp.maximum(offset, 0).astype(f32) * rate), 0.0)
    place = lax.broadcasted_iota(jnp.int32, (size, 1), 0)
    ahead = jnp.exp((place + 1).astype(f32) * rate)
    behind = jnp.exp((size - 1 - place).astype(f32) * rate)
    return decay, ahead, behind


def forward_kernel(cores, team, order, firsts, lasts, before_group, floats, *refs):
    qkv_refs = refs[:cores]
    col_ref, row_ref, start_ref, normed_ref, scale_ref, states_ref, state = refs[cores:]
    step = pl.program_id(0)
    rank = step
    at = order[rank]
    rate = floats[0]

    @pl.when(step == 0)
    def _():
        state[...] = start_ref[...].astype(f32)

    qkv = chosen(qkv_refs, (at, team))
    query, key, value = qkv[:, :KEY], qkv[:, KEY : 2 * KEY], qkv[:, 2 * KEY :]
    seg = col_ref[...]
    grown = jnp.exp(jnp.full((1, 1), 1.0, f32) * floats[1])
    decay, ahead, behind = weights_of(rate, seg, row_ref[0])
    first, last = firsts[at], lasts[at]
    before = jnp.where(rank == 0, before_group[0], lasts[order[jnp.maximum(rank - 1, 0)]])
    ahead = jnp.where((seg == first) & (before == first), ahead, 0.0)
    behind = jnp.where(seg == last, behind, 0.0)
    carry = jnp.where((before == first) & (first == last), grown, 0.0)
    held = state[...].astype(bf16)
    states_ref[0] = held
    scores = dot(query, key, 1, 1)
    weights = (scores * decay).astype(bf16)
    mixed = dot(weights, value) + ahead * dot(query, held)
    scale = lax.rsqrt(jnp.mean(mixed * mixed, axis=-1, keepdims=True) + eps_group)
    normed_ref[...] = mixed * scale
    scale_ref[...] = scale
    state[...] = dot((key * behind).astype(bf16), value, 0, 0) + carry * state[...]


def backward_kernel(cores, team, order, firsts, lasts, before_group, floats, *refs):
    groups = [refs[i * cores : (i + 1) * cores] for i in range(4)]
    qkv_refs, mixed_refs, rest_refs, gate_refs = groups
    states_ref, col_ref, row_ref, start_ref, out_ref, state = refs[4 * cores :]
    step = pl.program_id(0)
    rank = pl.num_programs(0) - 1 - step
    at = order[rank]
    rate = floats[0]

    @pl.when(step == 0)
    def _():
        state[...] = start_ref[...].astype(f32)

    qkv = chosen(qkv_refs, (at, team))
    grad = chosen(mixed_refs, (at, team))
    query, key, value = qkv[:, :KEY], qkv[:, KEY : 2 * KEY], qkv[:, 2 * KEY :]
    seg = col_ref[...]
    grown = jnp.exp(jnp.full((1, 1), 1.0, f32) * floats[1])
    decay, ahead, behind = weights_of(rate, seg, row_ref[0])
    first, last = firsts[at], lasts[at]
    before = jnp.where(rank == 0, before_group[0], lasts[order[jnp.maximum(rank - 1, 0)]])
    ahead = jnp.where((seg == first) & (before == first), ahead, 0.0)
    behind = jnp.where(seg == last, behind, 0.0)
    carry = jnp.where((before == first) & (first == last), grown, 0.0)
    held = state[...].astype(bf16)
    weights = (dot(query, key, 1, 1) * decay).astype(bf16)
    grad_rest = chosen(rest_refs, (at, team))
    grad_weights = dot(grad, value, 1, 1) + dot(grad_rest, value, 1, 1)
    grad_scores = (grad_weights * decay).astype(bf16)
    grad_query = dot(grad_scores, key) + ahead * dot(grad, states_ref[0], 1, 1)
    grad_key = dot(grad_scores, query, 0, 0) + behind * dot(value, held, 1, 1)
    grad_value = dot(weights, grad, 0, 0) + behind * dot(key, held)
    out_ref[:, :KEY] = grad_query.astype(bf16)
    out_ref[:, KEY : 2 * KEY] = grad_key.astype(bf16)
    out_ref[:, 2 * KEY : 2 * KEY + VALUE] = grad_value.astype(bf16)
    out_ref[:, 2 * KEY + VALUE :] = chosen(gate_refs, (at, team))
    state[...] = dot((query * ahead).astype(bf16), grad, 0, 0) + carry * state[...]


def walk(kernel, cores, team, edges, split, whole, outs, reverse, flops, moved):
    chunks = cores * team

    def at(step, order):
        return order[chunks - 1 - step] if reverse else order[step]

    def block(e, width, size):
        return pl.BlockSpec(
            (size, width),
            lambda i, order, *_: (jnp.clip(at(i, order) - e * team, 0, team - 1), 0),
        )

    def spec(shape, each):
        zeros = (0,) * (len(shape) - 1)
        if each:
            return pl.BlockSpec(shape, lambda i, order, *_: (at(i, order),) + zeros)
        return pl.BlockSpec(shape, lambda i, order, *_: (0,) + zeros)

    arrays, specs = [], []
    for group in split:
        for e, array in enumerate(group):
            arrays.append(array)
            specs.append(block(e, array.shape[1], array.shape[0] // team))
    for array, shape, each in whole:
        arrays.append(array)
        specs.append(spec(shape, each))
    return pl.pallas_call(
        partial(kernel, cores, team),
        grid_spec=pltpu.PrefetchScalarGridSpec(
            num_scalar_prefetch=len(edges),
            grid=(chunks,),
            in_specs=specs,
            out_specs=[spec(shape, each) for _, shape, each in outs],
            scratch_shapes=[pltpu.VMEM((KEY, VALUE), f32)],
        ),
        out_shape=[shape for shape, _, _ in outs],
        compiler_params=pltpu.CompilerParams(dimension_semantics=("arbitrary",)),
        cost_estimate=pl.CostEstimate(flops=flops, bytes_accessed=moved, transcendentals=0),
    )(*edges, *arrays)


def gate_back_kernel(grad_ref, weight_ref, gate_ref, normed_ref, scale_ref, gate_out, mixed_out, rest_out):
    for at in blocks_of(grad_ref):
        grad_gated = dot(grad_ref[at], weight_ref[...])
        gate = gate_ref[at]
        normed = normed_ref[at]
        sigmoid = 1.0 / (1.0 + jnp.exp(-gate))
        gate_out[at] = (
            grad_gated * normed * (sigmoid + gate * sigmoid * (1.0 - sigmoid))
        ).astype(bf16)
        grad_normed = grad_gated * (gate * sigmoid)
        along = jnp.mean(grad_normed * normed, axis=-1, keepdims=True)
        grad_mixed = scale_ref[at] * (grad_normed - normed * along)
        rounded = grad_mixed.astype(bf16)
        mixed_out[at] = rounded
        rest_out[at] = (grad_mixed - rounded.astype(f32)).astype(bf16)


def gate_back(grad, weight, gate, normed, scale, e):
    rows, width = grad.shape
    size = min(256, rows)
    steps = rows // size
    own = lambda i: (i, 0)
    far = lambda i: (e * steps + i, 0)
    shape = jax.ShapeDtypeStruct((rows, VALUE), bf16)
    return pl.pallas_call(
        gate_back_kernel,
        grid=(steps,),
        in_specs=[
            pl.BlockSpec((size, width), own),
            pl.BlockSpec(weight.shape, lambda i: (0, 0)),
            pl.BlockSpec((size, VALUE), own),
            pl.BlockSpec((size, VALUE), far),
            pl.BlockSpec((size, 1), far),
        ],
        out_specs=[pl.BlockSpec((size, VALUE), own)] * 3,
        out_shape=[shape] * 3,
        compiler_params=pltpu.CompilerParams(dimension_semantics=("arbitrary",)),
        cost_estimate=pl.CostEstimate(
            flops=2 * rows * width * VALUE, bytes_accessed=2 * rows * width, transcendentals=0
        ),
    )(grad, weight, gate, normed, scale)


def shards(tokens, norm_gains, w_mixer, w_out, w_up, w_down, seg_ids, cotangent):
    team, _, cores = (lax.axis_size(a) for a in ("team", "group", "head"))
    _, j, c = (lax.axis_index(a) for a in ("group", "team", "head"))
    heads_here = w_mixer.shape[2]
    length, _ = tokens.shape
    size = length // cores
    chunks = team
    near = range(cores)
    units = w_up.shape[2] // team

    rows_here = w_mixer.shape[1]
    mixer_slabs = w_mixer[0].transpose(1, 0, 2)
    rest = jnp.concatenate(
        [
            w_out[0].reshape(team, VALUE, rows_here).transpose(0, 2, 1),
            w_up[0].reshape(rows_here, team, units).transpose(1, 0, 2),
            w_down[0].reshape(team, units, rows_here).transpose(0, 2, 1),
        ],
        axis=2,
    )
    mixer_rows = join(deal(lambda m: lax.dynamic_index_in_dim(mixer_slabs, m, 0, keepdims=False)))
    whole = partial(lax.all_gather, axis_name="group", axis=0, tiled=True)
    w_mixer_all = whole(mixer_rows)

    segs = [seg_ids] + [swap(seg_ids, "team", d) for d in range(1, team)]
    seg = jnp.stack(
        [
            lax.dynamic_slice_in_dim(segs[d], (c ^ e) * size, size, 0)
            for e in near
            for d in range(team)
        ]
    )
    chunks = cores * team
    rank = jnp.arange(chunks)
    order = (((rank % cores) ^ c) * team + ((rank // cores) ^ j)).astype(jnp.int32)
    place = jnp.stack([(j ^ d) * length + (c ^ e) * size for e in near for d in range(team)])
    group_length = team * length
    group_first = jnp.min(seg, keepdims=True)
    group_last = jnp.max(seg, keepdims=True)
    before_group = shift(group_last + 1, 1) - 1
    head = c * heads_here + j
    rate = jnp.log1p(-jnp.exp2(-5.0 - head.astype(f32)))
    floats = rate * jnp.array([1.0, size], f32)
    seg_col = seg.reshape(-1, 1)
    seg_row = seg[:, None, :]
    token = (place[:, None] + jnp.arange(size)).reshape(-1, 1)
    to_end = jnp.where(
        seg_col == group_last, jnp.exp((group_length - 1 - token).astype(f32) * rate), 0.0
    )
    from_start = jnp.where(
        seg_col == before_group, jnp.exp((token + 1).astype(f32) * rate), 0.0
    )
    through = jnp.where(
        (before_group == group_first) & (group_first == group_last),
        jnp.exp(group_length * rate),
        0.0,
    )
    edges = (order, seg[:, 0], seg[:, size - 1], before_group.reshape(1), floats)
    hops = -(-(SEQ_MOST - 1) // group_length)
    rows = team * size

    def here(value, e):
        return value[e * rows : (e + 1) * rows]

    def state_sum(left, factor, right):
        return sum(
            dot((left[e] * here(factor, e)).astype(bf16), right[e], 0, 0) for e in near
        )

    def passed(value, steps):
        state = shift(value.astype(bf16), steps)
        for _ in range(hops - 1):
            state = shift((value + through * state.astype(f32)).astype(bf16), steps)
        return state

    gain_one, gain_two = norm_gains[0, 0], norm_gains[0, 1]
    stream = lax.dynamic_slice_in_dim(tokens, c * size, size, 0).astype(f32)
    cot = lax.dynamic_slice_in_dim(cotangent, c * size, size, 0)
    hidden_own, normed1, scaled1 = layer_norm(stream, gain_one)
    hidden = share(after(hidden_own.astype(bf16), mixer_rows))
    rest = after(rest, mixer_rows)
    rest_rows = join(deal(lambda m: lax.dynamic_index_in_dim(rest, m, 0, keepdims=False)))
    w_o = whole(rest_rows[:, :VALUE])
    w_ud = whole(rest_rows[:, VALUE:])
    cot_all = share(after(cot, hidden[0]))

    qkv = [dot(h, w_mixer_all[:, : 2 * KEY + VALUE]).astype(bf16) for h in hidden]
    end_state = state_sum(
        [v[:, KEY : 2 * KEY] for v in qkv], to_end, [v[:, 2 * KEY :] for v in qkv]
    )
    chunk_flops = 2 * size * size * (KEY + VALUE) + 4 * size * KEY * VALUE
    state_in = passed(end_state, 1)
    normed, scale, states = walk(
        forward_kernel,
        cores,
        team,
        edges,
        [qkv],
        [
            (seg_col, (size, 1), True),
            (seg_row, (1, 1, size), True),
            (state_in, (KEY, VALUE), False),
        ],
        [
            (jax.ShapeDtypeStruct((chunks * size, VALUE), f32), (size, VALUE), True),
            (jax.ShapeDtypeStruct((chunks * size, 1), f32), (size, 1), True),
            (jax.ShapeDtypeStruct((chunks, KEY, VALUE), bf16), (1, KEY, VALUE), True),
        ],
        False,
        chunks * chunk_flops,
        chunks * size * 4096,
    )
    gate = [dot(h, w_mixer_all[:, 2 * KEY + VALUE :]) for h in hidden]
    gate = after(gate, state_in)
    gated = []
    for e in near:
        gated.append(
            (gate[e] * jax.nn.sigmoid(gate[e]) * here(normed, e)).astype(bf16)
        )
    stream = stream + reduce(gated, w_o, 0)[0]

    hidden2_own, normed2, scaled2 = layer_norm(stream, gain_two)
    hidden2 = share(hidden2_own.astype(bf16))
    grad_act = [dot(t, w_ud[:, units:]) for t in cot_all]
    pairs = []
    for e in near:
        pairs.append(unit_step(hidden2[e], w_ud, grad_act[e], units))
    act, grad_up = [p[0] for p in pairs], [p[1] for p in pairs]

    def both_cores(rows):
        rows = rows.astype(bf16)
        got = [rows] + [swap(rows, "head", e) for e in range(1, cores)]
        return join(straight(got, "head"))

    grad_hidden2, sent = reduce(grad_up, w_ud, 0)
    down_done = grads(after(cot_all, sent), act)
    up_done = grads(after(hidden2, sent), grad_up)
    norm_part, gain_grad_two = norm_back(grad_hidden2, normed2, scaled2, gain_two)
    grad = cot.astype(f32) + norm_part
    grad_all = share(grad.astype(bf16))
    out_done = grads(grad_all, gated)
    backs = []
    for e in near:
        backs.append(gate_back(grad_all[e], w_o, gate[e], normed, scale, e))
    grad_gate, grad_mixed, mixed_rest = ([v[i] for v in backs] for i in range(3))
    gate_done = grads(hidden, grad_gate)
    grad_before = state_sum([v[:, :KEY] for v in qkv], from_start, grad_mixed)
    grad_in = passed(grad_before, -1)
    stream = stream + reduce(after(act, grad_before), w_ud, 1)[0]
    (proj,) = walk(
        backward_kernel,
        cores,
        team,
        edges,
        [qkv, grad_mixed, mixed_rest, grad_gate],
        [
            (states, (1, KEY, VALUE), True),
            (seg_col, (size, 1), True),
            (seg_row, (1, 1, size), True),
            (grad_in, (KEY, VALUE), False),
        ],
        [
            (
                jax.ShapeDtypeStruct((chunks * size, 2 * KEY + 2 * VALUE), bf16),
                (size, 2 * KEY + 2 * VALUE),
                True,
            ),
        ],
        True,
        3 * chunks * chunk_flops,
        chunks * size * 12000,
    )
    grad_proj = [here(proj, e) for e in near]
    qkv_done = grads(hidden, [v[:, : 2 * KEY + VALUE] for v in grad_proj])
    grad_hidden = reduce(grad_proj, w_mixer_all, 0)[0]
    output = both_cores(stream)
    norm_part, gain_grad_one = norm_back(grad_hidden, normed1, scaled1, gain_one)
    input_grad = both_cores(grad + norm_part)
    gain_grad = total(jnp.stack([gain_grad_one, gain_grad_two]))

    def own_rows(done):
        return deal(lambda m: lax.dynamic_slice_in_dim(done, m * rows_here, rows_here, 0))

    own_units = own_rows(jnp.concatenate([up_done, down_done], axis=1))
    own_heads = own_rows(jnp.concatenate([out_done, gate_done], axis=1))
    own_qkv = own_rows(qkv_done)
    mixer_grad = jnp.concatenate(
        [
            jnp.stack(own_qkv, axis=1),
            jnp.stack([v[:, VALUE:] for v in own_heads], axis=1),
        ],
        axis=-1,
    ).astype(f32)
    up_grad = jnp.concatenate([v[:, :units] for v in own_units], axis=1).astype(f32)
    down_grad = jnp.concatenate([v[:, units:].T for v in own_units], axis=0).astype(f32)
    out_grad = jnp.concatenate([v[:, :VALUE].T for v in own_heads], axis=0).astype(f32)
    return (
        output,
        input_grad,
        gain_grad[None],
        mixer_grad[None],
        out_grad[None],
        up_grad[None],
        down_grad[None],
    )


def solution(mesh):
    devices, cores = mesh.devices.shape
    team = team_size(devices, HEADS // cores)
    fine = Mesh(mesh.devices.reshape(devices // team, team, cores), ("group", "team", "head"))
    fsdp = ("group", "team")

    return jax.shard_map(
        shards,
        mesh=fine,
        in_specs=(
            P(fsdp, None),
            P(),
            P(None, fsdp, "head", None),
            P(None, "head", fsdp),
            P(None, fsdp, "head"),
            P(None, "head", fsdp),
            P(fsdp),
            P(fsdp, None),
        ),
        out_specs=(
            P(fsdp, None),
            P(fsdp, None),
            P(),
            P(None, fsdp, "head", None),
            P(None, "head", fsdp),
            P(None, fsdp, "head"),
            P(None, "head", fsdp),
        ),
        check_vma=False,
    )
```

```python
from functools import partial

import jax
import jax.numpy as jnp
from jax import lax
from jax.experimental import pallas as pl
from jax.experimental.pallas import tpu as pltpu
from jax.sharding import Mesh, PartitionSpec as P


HEADS = 8
KEY = 256
VALUE = 512
SEQ_MOST = 2048

eps_norm = 1e-05
eps_group = 1e-06
bf16 = jnp.bfloat16
f32 = jnp.float32


def team_size(devices, heads_here):
    team = 4
    while heads_here % team or devices % team:
        team //= 2
    return team


def dot(a, b, left=1, right=0):
    return lax.dot_general(a, b, (((left,), (right,)), ((), ())), preferred_element_type=f32)


def layer_norm(stream, gain):
    centered = stream - jnp.mean(stream, axis=-1, keepdims=True)
    scaled = lax.rsqrt(jnp.mean(centered * centered, axis=-1, keepdims=True) + eps_norm)
    normed = centered * scaled
    return (normed * gain, normed, scaled)


def norm_back(grad_out, normed, scaled, gain):
    grad_norm = grad_out * gain
    inner = jnp.mean(grad_norm, axis=-1, keepdims=True)
    along = jnp.mean(grad_norm * normed, axis=-1, keepdims=True)
    return (scaled * (grad_norm - inner - normed * along), jnp.sum(grad_out * normed, axis=0))


def swap(value, axis, d):
    count = lax.axis_size(axis)
    return lax.ppermute(value, axis, [(i, i ^ d) for i in range(count)])


def shift(value, steps):
    count = lax.axis_size("g")
    pairs = [(i, i + steps) for i in range(count) if 0 <= i + steps < count]
    return lax.ppermute(value, "g", pairs)


def total(value):
    for axis in ("h", "t", "g"):
        parts = [value] + [swap(value, axis, d) for d in range(1, lax.axis_size(axis))]
        while len(parts) > 1:
            parts = [parts[k] + parts[k + 1] for k in range(0, len(parts), 2)]
        value = parts[0]
    return value


def straight(pieces, axis):
    mine = lax.axis_index(axis)
    pieces = list(pieces)
    bit = 1
    while bit < len(pieces):
        odd = (mine & bit) != 0
        pieces = [jnp.where(odd, pieces[i ^ bit], pieces[i]) for i in range(len(pieces))]
        bit *= 2
    return pieces


def deal(pick):
    mine = lax.axis_index("t")
    got = [pick(mine)]
    for d in range(1, lax.axis_size("t")):
        got.append(swap(pick(mine ^ d), "t", d))
    return straight(got, "t")


def join(parts):
    rows = parts[0].shape[0]
    out = jnp.zeros((rows * len(parts),) + parts[0].shape[1:], parts[0].dtype)
    for i, part in enumerate(parts):
        out = lax.dynamic_update_slice_in_dim(out, part, i * rows, 0)
    return out


def share(own):
    parts = [own] + [swap(own, "t", d) for d in range(1, lax.axis_size("t"))]
    rows = join(parts)
    return [rows] + [swap(rows, "h", e) for e in range(1, lax.axis_size("h"))]


def after(values, first):
    return lax.optimization_barrier((values, first))[0]


def reduce_kernel(team, rows_ref, weight_ref, *refs):
    others, outs = refs[: len(refs) - team], refs[len(refs) - team :]
    total = dot(rows_ref[...], weight_ref[...], 1, 1)
    for other in others:
        total = total + other[...].astype(f32)
    piece = total.shape[0] // team
    for d, out in enumerate(outs):
        out[...] = total[d * piece : (d + 1) * piece].astype(out.dtype)


def reduce(rows, weight, column, stack=None):
    team, cores = lax.axis_size("t"), len(rows)
    count, depth = rows[0].shape
    width = weight.shape[0]
    step = min(1024 if depth <= 512 else 512, width)
    part = weight[:, column * depth : (column + 1) * depth]
    first = [dot(rows[e], part, 1, 1).astype(bf16) for e in range(1, cores)]
    others = [swap(v, "h", e) for e, v in enumerate(first, 1)]
    piece = count // team
    out = pl.pallas_call(
        partial(reduce_kernel, team),
        grid=(width // step,),
        in_specs=[
            pl.BlockSpec((count, depth), lambda i: (0, 0)),
            pl.BlockSpec((step, depth), lambda i: (i, column)),
        ]
        + [pl.BlockSpec((count, step), lambda i: (0, i))] * (cores - 1),
        out_specs=[pl.BlockSpec((piece, step), lambda i: (0, i))] * team,
        out_shape=[jax.ShapeDtypeStruct((piece, width), bf16 if d else f32) for d in range(team)],
        cost_estimate=pl.CostEstimate(
            flops=2 * count * depth * width,
            bytes_accessed=2 * width * (depth + 2 * count),
            transcendentals=0,
        ),
    )(rows[0] if stack is None else stack, weight, *others)
    got = [swap(out[d], "t", d) for d in range(1, team)]
    value = out[0]
    for v in got:
        value = value + v.astype(f32)
    return value, out


def grads(left, right):
    value = dot(left[0], right[0], 0, 0)
    for a, b in zip(left[1:], right[1:]):
        value = value + dot(a, b, 0, 0)
    value = value.astype(bf16)
    return lax.psum_scatter(value, "g", scatter_dimension=0, tiled=True)


SUB = 128


def blocks_of(ref):
    size = min(SUB, ref.shape[0])
    return [slice(i, i + size) for i in range(0, ref.shape[0], size)]


def unit_kernel(hidden_ref, weight_ref, grad_ref, act_out, grad_out):
    for at in blocks_of(hidden_ref):
        value = dot(hidden_ref[at], weight_ref[...])
        cumulative = 0.5 + 0.5 * lax.erf(value * (0.5**0.5))
        density = jnp.exp(-0.5 * value * value) * 0.3989422804014327
        act_out[at] = (value * cumulative).astype(bf16)
        grad_out[at] = (grad_ref[at] * (cumulative + value * density)).astype(bf16)


def unit_step(hidden, weight, grad, units):
    rows, width = hidden.shape
    size = min(256, rows)
    own = lambda i: (i, 0)
    shape = jax.ShapeDtypeStruct((rows, units), bf16)
    return pl.pallas_call(
        unit_kernel,
        grid=(rows // size,),
        in_specs=[
            pl.BlockSpec((size, width), own),
            pl.BlockSpec((width, units), lambda i: (0, 0)),
            pl.BlockSpec((size, units), own),
        ],
        out_specs=[pl.BlockSpec((size, units), own)] * 2,
        out_shape=[shape] * 2,
        cost_estimate=pl.CostEstimate(
            flops=2 * rows * width * units, bytes_accessed=2 * rows * width, transcendentals=0
        ),
    )(hidden, weight, grad)


def chosen(refs, at):
    team = at[1]
    value = refs[0][...]
    for e in range(1, len(refs)):
        value = jnp.where(at[0] >= e * team, refs[e][...], value)
    return value


def weights_of(rate, seg_col, seg_row):
    size = seg_col.shape[0]
    row = lax.broadcasted_iota(jnp.int32, (size, size), 0)
    col = lax.broadcasted_iota(jnp.int32, (size, size), 1)
    offset = row - col
    valid = (offset >= 0) & (seg_col == seg_row)
    decay = jnp.where(valid, jnp.exp(jnp.maximum(offset, 0).astype(f32) * rate), 0.0)
    place = lax.broadcasted_iota(jnp.int32, (size, 1), 0)
    ahead = jnp.exp((place + 1).astype(f32) * rate)
    behind = jnp.exp((size - 1 - place).astype(f32) * rate)
    return decay, ahead, behind


def forward_kernel(cores, team, order, firsts, lasts, before_group, floats, *refs):
    qkv_refs = refs[:cores]
    col_ref, row_ref, start_ref, normed_ref, scale_ref, states_ref, state = refs[cores:]
    step = pl.program_id(0)
    rank = step
    at = order[rank]
    rate = floats[0]

    @pl.when(step == 0)
    def _():
        state[...] = start_ref[...].astype(f32)

    qkv = chosen(qkv_refs, (at, team))
    query, key, value = qkv[:, :KEY], qkv[:, KEY : 2 * KEY], qkv[:, 2 * KEY :]
    seg = col_ref[...]
    grown = jnp.exp(jnp.full((1, 1), 1.0, f32) * floats[1])
    decay, ahead, behind = weights_of(rate, seg, row_ref[0])
    first, last = firsts[at], lasts[at]
    before = jnp.where(rank == 0, before_group[0], lasts[order[jnp.maximum(rank - 1, 0)]])
    ahead = jnp.where((seg == first) & (before == first), ahead, 0.0)
    behind = jnp.where(seg == last, behind, 0.0)
    carry = jnp.where((before == first) & (first == last), grown, 0.0)
    held = state[...].astype(bf16)
    states_ref[0] = held
    scores = dot(query, key, 1, 1)
    weights = (scores * decay).astype(bf16)
    mixed = dot(weights, value) + ahead * dot(query, held)
    scale = lax.rsqrt(jnp.mean(mixed * mixed, axis=-1, keepdims=True) + eps_group)
    normed_ref[...] = mixed * scale
    scale_ref[...] = scale
    state[...] = dot((key * behind).astype(bf16), value, 0, 0) + carry * state[...]


def backward_kernel(cores, team, order, firsts, lasts, before_group, floats, *refs):
    groups = [refs[i * cores : (i + 1) * cores] for i in range(4)]
    qkv_refs, mixed_refs, rest_refs, gate_refs = groups
    states_ref, col_ref, row_ref, start_ref, out_ref, state = refs[4 * cores :]
    step = pl.program_id(0)
    rank = pl.num_programs(0) - 1 - step
    at = order[rank]
    rate = floats[0]

    @pl.when(step == 0)
    def _():
        state[...] = start_ref[...].astype(f32)

    qkv = chosen(qkv_refs, (at, team))
    grad = chosen(mixed_refs, (at, team))
    query, key, value = qkv[:, :KEY], qkv[:, KEY : 2 * KEY], qkv[:, 2 * KEY :]
    seg = col_ref[...]
    grown = jnp.exp(jnp.full((1, 1), 1.0, f32) * floats[1])
    decay, ahead, behind = weights_of(rate, seg, row_ref[0])
    first, last = firsts[at], lasts[at]
    before = jnp.where(rank == 0, before_group[0], lasts[order[jnp.maximum(rank - 1, 0)]])
    ahead = jnp.where((seg == first) & (before == first), ahead, 0.0)
    behind = jnp.where(seg == last, behind, 0.0)
    carry = jnp.where((before == first) & (first == last), grown, 0.0)
    held = state[...].astype(bf16)
    weights = (dot(query, key, 1, 1) * decay).astype(bf16)
    grad_rest = chosen(rest_refs, (at, team))
    grad_weights = dot(grad, value, 1, 1) + dot(grad_rest, value, 1, 1)
    grad_scores = (grad_weights * decay).astype(bf16)
    grad_query = dot(grad_scores, key) + ahead * dot(grad, states_ref[0], 1, 1)
    grad_key = dot(grad_scores, query, 0, 0) + behind * dot(value, held, 1, 1)
    grad_value = dot(weights, grad, 0, 0) + behind * dot(key, held)
    out_ref[:, :KEY] = grad_query.astype(bf16)
    out_ref[:, KEY : 2 * KEY] = grad_key.astype(bf16)
    out_ref[:, 2 * KEY : 2 * KEY + VALUE] = grad_value.astype(bf16)
    out_ref[:, 2 * KEY + VALUE :] = chosen(gate_refs, (at, team))
    state[...] = dot((query * ahead).astype(bf16), grad, 0, 0) + carry * state[...]


def walk(kernel, cores, team, edges, split, whole, outs, reverse, flops, moved):
    chunks = cores * team

    def at(step, order):
        return order[chunks - 1 - step] if reverse else order[step]

    def block(e, width, size):
        return pl.BlockSpec(
            (size, width),
            lambda i, order, *_: (jnp.clip(at(i, order) - e * team, 0, team - 1), 0),
        )

    def spec(shape, each):
        zeros = (0,) * (len(shape) - 1)
        if each:
            return pl.BlockSpec(shape, lambda i, order, *_: (at(i, order),) + zeros)
        return pl.BlockSpec(shape, lambda i, order, *_: (0,) + zeros)

    arrays, specs = [], []
    for group in split:
        for e, array in enumerate(group):
            arrays.append(array)
            specs.append(block(e, array.shape[1], array.shape[0] // team))
    for array, shape, each in whole:
        arrays.append(array)
        specs.append(spec(shape, each))
    return pl.pallas_call(
        partial(kernel, cores, team),
        grid_spec=pltpu.PrefetchScalarGridSpec(
            num_scalar_prefetch=len(edges),
            grid=(chunks,),
            in_specs=specs,
            out_specs=[spec(shape, each) for _, shape, each in outs],
            scratch_shapes=[pltpu.VMEM((KEY, VALUE), f32)],
        ),
        out_shape=[shape for shape, _, _ in outs],
        cost_estimate=pl.CostEstimate(flops=flops, bytes_accessed=moved, transcendentals=0),
    )(*edges, *arrays)


def gate_back_kernel(grad_ref, weight_ref, gate_ref, normed_ref, scale_ref, gate_out, mixed_out, rest_out):
    for at in blocks_of(grad_ref):
        grad_gated = dot(grad_ref[at], weight_ref[...])
        gate = gate_ref[at]
        normed = normed_ref[at]
        sigmoid = 1.0 / (1.0 + jnp.exp(-gate))
        gate_out[at] = (
            grad_gated * normed * (sigmoid + gate * sigmoid * (1.0 - sigmoid))
        ).astype(bf16)
        grad_normed = grad_gated * (gate * sigmoid)
        along = jnp.mean(grad_normed * normed, axis=-1, keepdims=True)
        grad_mixed = scale_ref[at] * (grad_normed - normed * along)
        rounded = grad_mixed.astype(bf16)
        mixed_out[at] = rounded
        rest_out[at] = (grad_mixed - rounded.astype(f32)).astype(bf16)


def gate_back(grad, weight, gate, normed, scale, e):
    rows, width = grad.shape
    size = min(256, rows)
    steps = rows // size
    own = lambda i: (i, 0)
    far = lambda i: (e * steps + i, 0)
    shape = jax.ShapeDtypeStruct((rows, VALUE), bf16)
    return pl.pallas_call(
        gate_back_kernel,
        grid=(steps,),
        in_specs=[
            pl.BlockSpec((size, width), own),
            pl.BlockSpec(weight.shape, lambda i: (0, 0)),
            pl.BlockSpec((size, VALUE), own),
            pl.BlockSpec((size, VALUE), far),
            pl.BlockSpec((size, 1), far),
        ],
        out_specs=[pl.BlockSpec((size, VALUE), own)] * 3,
        out_shape=[shape] * 3,
        cost_estimate=pl.CostEstimate(
            flops=2 * rows * width * VALUE, bytes_accessed=2 * rows * width, transcendentals=0
        ),
    )(grad, weight, gate, normed, scale)


def shards(tokens, norm_gains, w_mixer, w_out, w_up, w_down, seg_ids, cotangent):
    team, _, cores = (lax.axis_size(a) for a in ("t", "g", "h"))
    _, j, c = (lax.axis_index(a) for a in ("g", "t", "h"))
    heads_here = w_mixer.shape[2]
    length, _ = tokens.shape
    size = length // cores
    chunks = team
    near = range(cores)
    units = w_up.shape[2] // team

    rows_here = w_mixer.shape[1]
    mixer_slabs = w_mixer[0].transpose(1, 0, 2)
    rest = jnp.concatenate(
        [
            w_out[0].reshape(team, VALUE, rows_here).transpose(0, 2, 1),
            w_up[0].reshape(rows_here, team, units).transpose(1, 0, 2),
            w_down[0].reshape(team, units, rows_here).transpose(0, 2, 1),
        ],
        axis=2,
    )
    mixer_rows = join(deal(lambda m: lax.dynamic_index_in_dim(mixer_slabs, m, 0, keepdims=False)))
    whole = partial(lax.all_gather, axis_name="g", axis=0, tiled=True)
    w_mixer_all = whole(mixer_rows)

    segs = [seg_ids] + [swap(seg_ids, "t", d) for d in range(1, team)]
    seg = jnp.stack(
        [
            lax.dynamic_slice_in_dim(segs[d], (c ^ e) * size, size, 0)
            for e in near
            for d in range(team)
        ]
    )
    chunks = cores * team
    rank = jnp.arange(chunks)
    order = (((rank % cores) ^ c) * team + ((rank // cores) ^ j)).astype(jnp.int32)
    place = jnp.stack([(j ^ d) * length + (c ^ e) * size for e in near for d in range(team)])
    group_length = team * length
    group_first = jnp.min(seg, keepdims=True)
    group_last = jnp.max(seg, keepdims=True)
    before_group = shift(group_last + 1, 1) - 1
    head = c * heads_here + j
    rate = jnp.log1p(-jnp.exp2(-5.0 - head.astype(f32)))
    floats = rate * jnp.array([1.0, size], f32)
    seg_col = seg.reshape(-1, 1)
    seg_row = seg[:, None, :]
    token = (place[:, None] + jnp.arange(size)).reshape(-1, 1)
    to_end = jnp.where(
        seg_col == group_last, jnp.exp((group_length - 1 - token).astype(f32) * rate), 0.0
    )
    from_start = jnp.where(
        seg_col == before_group, jnp.exp((token + 1).astype(f32) * rate), 0.0
    )
    through = jnp.where(
        (before_group == group_first) & (group_first == group_last),
        jnp.exp(group_length * rate),
        0.0,
    )
    edges = (order, seg[:, 0], seg[:, size - 1], before_group.reshape(1), floats)
    hops = -(-(SEQ_MOST - 1) // group_length)
    rows = team * size

    def here(value, e):
        return value[e * rows : (e + 1) * rows]

    def state_sum(left, factor, right):
        return sum(
            dot((left[e] * here(factor, e)).astype(bf16), right[e], 0, 0) for e in near
        )

    def passed(value, steps):
        state = shift(value.astype(bf16), steps)
        for _ in range(hops - 1):
            state = shift((value + through * state.astype(f32)).astype(bf16), steps)
        return state

    gain_one, gain_two = norm_gains[0, 0], norm_gains[0, 1]
    stream = lax.dynamic_slice_in_dim(tokens, c * size, size, 0).astype(f32)
    cot = lax.dynamic_slice_in_dim(cotangent, c * size, size, 0)
    hidden_own, normed1, scaled1 = layer_norm(stream, gain_one)
    hidden = share(after(hidden_own.astype(bf16), mixer_rows))
    rest = after(rest, mixer_rows)
    rest_rows = join(deal(lambda m: lax.dynamic_index_in_dim(rest, m, 0, keepdims=False)))
    w_o = whole(rest_rows[:, :VALUE])
    w_ud = whole(rest_rows[:, VALUE:])
    cot_all = share(after(cot, hidden[0]))

    qkv = [dot(h, w_mixer_all[:, : 2 * KEY + VALUE]).astype(bf16) for h in hidden]
    end_state = state_sum(
        [v[:, KEY : 2 * KEY] for v in qkv], to_end, [v[:, 2 * KEY :] for v in qkv]
    )
    chunk_flops = 2 * size * size * (KEY + VALUE) + 4 * size * KEY * VALUE
    state_in = passed(end_state, 1)
    normed, scale, states = walk(
        forward_kernel,
        cores,
        team,
        edges,
        [qkv],
        [
            (seg_col, (size, 1), True),
            (seg_row, (1, 1, size), True),
            (state_in, (KEY, VALUE), False),
        ],
        [
            (jax.ShapeDtypeStruct((chunks * size, VALUE), f32), (size, VALUE), True),
            (jax.ShapeDtypeStruct((chunks * size, 1), f32), (size, 1), True),
            (jax.ShapeDtypeStruct((chunks, KEY, VALUE), bf16), (1, KEY, VALUE), True),
        ],
        False,
        chunks * chunk_flops,
        chunks * size * 4096,
    )
    gate = [dot(h, w_mixer_all[:, 2 * KEY + VALUE :]) for h in hidden]
    gate = after(gate, state_in)
    gated = []
    for e in near:
        gated.append(
            (gate[e] * jax.nn.sigmoid(gate[e]) * here(normed, e)).astype(bf16)
        )
    stream = stream + reduce(gated, w_o, 0)[0]

    hidden2_own, normed2, scaled2 = layer_norm(stream, gain_two)
    hidden2 = share(hidden2_own.astype(bf16))
    grad_act = [dot(t, w_ud[:, units:]) for t in cot_all]
    pairs = []
    for e in near:
        pairs.append(unit_step(hidden2[e], w_ud, grad_act[e], units))
    act, grad_up = [p[0] for p in pairs], [p[1] for p in pairs]

    def both_cores(rows):
        rows = rows.astype(bf16)
        got = [rows] + [swap(rows, "h", e) for e in range(1, cores)]
        return join(straight(got, "h"))

    grad_hidden2, sent = reduce(grad_up, w_ud, 0)
    down_done = grads(after(cot_all, sent), act)
    up_done = grads(after(hidden2, sent), grad_up)
    norm_part, gain_grad_two = norm_back(grad_hidden2, normed2, scaled2, gain_two)
    grad = cot.astype(f32) + norm_part
    grad_all = share(grad.astype(bf16))
    out_done = grads(grad_all, gated)
    backs = []
    for e in near:
        backs.append(gate_back(grad_all[e], w_o, gate[e], normed, scale, e))
    grad_gate, grad_mixed, mixed_rest = ([v[i] for v in backs] for i in range(3))
    gate_done = grads(hidden, grad_gate)
    grad_before = state_sum([v[:, :KEY] for v in qkv], from_start, grad_mixed)
    grad_in = passed(grad_before, -1)
    added = reduce(after(act, grad_before), w_ud, 1)[0]
    (proj,) = walk(
        backward_kernel,
        cores,
        team,
        edges,
        [qkv, grad_mixed, mixed_rest, grad_gate],
        [
            (states, (1, KEY, VALUE), True),
            (seg_col, (size, 1), True),
            (seg_row, (1, 1, size), True),
            (grad_in, (KEY, VALUE), False),
        ],
        [
            (
                jax.ShapeDtypeStruct((chunks * size, 2 * KEY + 2 * VALUE), bf16),
                (size, 2 * KEY + 2 * VALUE),
                True,
            ),
        ],
        True,
        3 * chunks * chunk_flops,
        chunks * size * 12000,
    )
    grad_proj = [here(proj, e) for e in near]
    qkv_done = grads(hidden, [v[:, : 2 * KEY + VALUE] for v in grad_proj])
    grad_hidden = reduce(grad_proj, w_mixer_all, 0, proj)[0]
    output = both_cores(stream + added)
    norm_part, gain_grad_one = norm_back(grad_hidden, normed1, scaled1, gain_one)
    input_grad = both_cores(grad + norm_part)
    gain_grad = total(jnp.stack([gain_grad_one, gain_grad_two]))

    def own_rows(done):
        return deal(lambda m: lax.dynamic_slice_in_dim(done, m * rows_here, rows_here, 0))

    own_units = own_rows(jnp.concatenate([up_done, down_done], axis=1))
    own_heads = own_rows(jnp.concatenate([out_done, gate_done], axis=1))
    own_qkv = own_rows(qkv_done)
    mixer_grad = jnp.concatenate(
        [
            jnp.stack(own_qkv, axis=1),
            jnp.stack([v[:, VALUE:] for v in own_heads], axis=1),
        ],
        axis=-1,
    ).astype(f32)
    up_grad = jnp.concatenate([v[:, :units] for v in own_units], axis=1).astype(f32)
    down_grad = jnp.concatenate([v[:, units:].T for v in own_units], axis=0).astype(f32)
    out_grad = jnp.concatenate([v[:, :VALUE].T for v in own_heads], axis=0).astype(f32)
    return (
        output,
        input_grad,
        gain_grad[None],
        mixer_grad[None],
        out_grad[None],
        up_grad[None],
        down_grad[None],
    )


def solution(mesh):
    devices, cores = mesh.devices.shape
    team = team_size(devices, HEADS // cores)
    fine = Mesh(mesh.devices.reshape(devices // team, team, cores), ("g", "t", "h"))
    fsdp = ("g", "t")

    return jax.shard_map(
        shards,
        mesh=fine,
        in_specs=(
            P(fsdp, None),
            P(),
            P(None, fsdp, "h", None),
            P(None, "h", fsdp),
            P(None, fsdp, "h"),
            P(None, "h", fsdp),
            P(fsdp),
            P(fsdp, None),
        ),
        out_specs=(
            P(fsdp, None),
            P(fsdp, None),
            P(),
            P(None, fsdp, "h", None),
            P(None, "h", fsdp),
            P(None, fsdp, "h"),
            P(None, "h", fsdp),
        ),
        check_vma=False,
    )
```

```python
from functools import partial

import jax
import jax.numpy as jnp
from jax import lax
from jax.experimental import pallas as pl
from jax.experimental.pallas import tpu as pltpu
from jax.sharding import Mesh, PartitionSpec as P


HEADS = 8
KEY = 256
VALUE = 512
SEQ_MOST = 2048

eps_norm = 1e-05
eps_group = 1e-06
bf16 = jnp.bfloat16
f32 = jnp.float32


def team_size(devices, heads_here):
    team = 4
    while heads_here % team or devices % team:
        team //= 2
    return team


def dot(a, b, left=1, right=0):
    return lax.dot_general(a, b, (((left,), (right,)), ((), ())), preferred_element_type=f32)


def layer_norm(stream, gain):
    centered = stream - jnp.mean(stream, axis=-1, keepdims=True)
    scaled = lax.rsqrt(jnp.mean(centered * centered, axis=-1, keepdims=True) + eps_norm)
    normed = centered * scaled
    return (normed * gain, normed, scaled)


def norm_back(grad_out, normed, scaled, gain):
    grad_norm = grad_out * gain
    inner = jnp.mean(grad_norm, axis=-1, keepdims=True)
    along = jnp.mean(grad_norm * normed, axis=-1, keepdims=True)
    return (scaled * (grad_norm - inner - normed * along), jnp.sum(grad_out * normed, axis=0))


def swap(value, axis, d):
    count = lax.axis_size(axis)
    return lax.ppermute(value, axis, [(i, i ^ d) for i in range(count)])


def shift(value, steps):
    count = lax.axis_size("g")
    pairs = [(i, i + steps) for i in range(count) if 0 <= i + steps < count]
    return lax.ppermute(value, "g", pairs)


def total(value):
    for axis in ("h", "t", "g"):
        parts = [value] + [swap(value, axis, d) for d in range(1, lax.axis_size(axis))]
        while len(parts) > 1:
            parts = [parts[k] + parts[k + 1] for k in range(0, len(parts), 2)]
        value = parts[0]
    return value


def straight(pieces, axis):
    mine = lax.axis_index(axis)
    pieces = list(pieces)
    bit = 1
    while bit < len(pieces):
        odd = (mine & bit) != 0
        pieces = [jnp.where(odd, pieces[i ^ bit], pieces[i]) for i in range(len(pieces))]
        bit *= 2
    return pieces


def deal(pick):
    mine = lax.axis_index("t")
    got = [pick(mine)]
    for d in range(1, lax.axis_size("t")):
        got.append(swap(pick(mine ^ d), "t", d))
    return straight(got, "t")


def join(parts):
    rows = parts[0].shape[0]
    out = jnp.zeros((rows * len(parts),) + parts[0].shape[1:], parts[0].dtype)
    for i, part in enumerate(parts):
        out = lax.dynamic_update_slice_in_dim(out, part, i * rows, 0)
    return out


def share(own, halves=False):
    parts = [own] + [swap(own, "t", d) for d in range(1, lax.axis_size("t"))]
    if halves:
        half = own.shape[0] // 2
        parts = [p[h * half : (h + 1) * half] for h in range(2) for p in parts]
    rows = join(parts)
    return [rows] + [swap(rows, "h", e) for e in range(1, lax.axis_size("h"))]


def after(values, first):
    return lax.optimization_barrier((values, first))[0]


def reduce_kernel(team, halves, rows_ref, weight_ref, *refs):
    others, outs = refs[: len(refs) - team], refs[len(refs) - team :]
    rows = rows_ref[...]
    total = dot(rows.reshape(-1, rows.shape[-1]), weight_ref[...], 1, 1)
    for other in others:
        total = total + other[...].astype(f32)
    piece = total.shape[0] // (team * halves)
    for d, out in enumerate(outs):
        for h in range(halves):
            at = (h * team + d) * piece
            out[h * piece : (h + 1) * piece] = total[at : at + piece].astype(out.dtype)


def other_kernel(rows_ref, weight_ref, out_ref):
    rows = rows_ref[...]
    out_ref[...] = dot(rows.reshape(-1, rows.shape[-1]), weight_ref[...], 1, 1).astype(bf16)


def reduce_half(rows, half, h, weight, column, first=None):
    team, cores = lax.axis_size("t"), len(rows)
    width = weight.shape[0]
    step = min(1024, width)

    def spec(value):
        depth = value.shape[-1]
        full = value.shape[0] != team * half
        value = value.reshape(team, -1, depth)
        return value, pl.BlockSpec((team, half, depth), lambda i: (0, h if full else 0, 0))

    def call(kernel, e, others, shapes):
        value, own = spec(rows[e])
        depth = value.shape[-1]
        return pl.pallas_call(
            kernel,
            grid=(width // step,),
            in_specs=[own, pl.BlockSpec((step, depth), lambda i: (i, column))]
            + [pl.BlockSpec((count, step), lambda i: (0, i)) for _ in others],
            out_specs=[pl.BlockSpec((s.shape[0], step), lambda i: (0, i)) for s in shapes],
            out_shape=shapes,
            cost_estimate=pl.CostEstimate(
                flops=2 * count * depth * width,
                bytes_accessed=2 * width * (depth + count),
                transcendentals=0,
            ),
        )(value, weight, *others)

    count = team * half
    shape = [jax.ShapeDtypeStruct((count, width), bf16)]
    mine = [call(other_kernel, e, [], shape)[0] for e in range(1, cores)]
    others = [swap(v, "h", e) for e, v in enumerate(mine, 1)]
    shapes = [jax.ShapeDtypeStruct((count // team, width), bf16 if d else f32) for d in range(team)]
    out = call(partial(reduce_kernel, team, 1), 0, others, shapes)
    got = [swap(out[d], "t", d) for d in range(1, team)]
    if first is not None:
        got = after(got, first)
    value = out[0]
    for v in got:
        value = value + v.astype(f32)
    return value, out


def reduce(rows, weight, column, stack=None, halves=1):
    team, cores = lax.axis_size("t"), len(rows)
    count, depth = rows[0].shape
    width = weight.shape[0]
    step = min(1024 if depth <= 512 else 512, width)
    part = weight[:, column * depth : (column + 1) * depth]
    first = [dot(rows[e], part, 1, 1).astype(bf16) for e in range(1, cores)]
    others = [swap(v, "h", e) for e, v in enumerate(first, 1)]
    piece = count // team
    out = pl.pallas_call(
        partial(reduce_kernel, team, halves),
        grid=(width // step,),
        in_specs=[
            pl.BlockSpec((count, depth), lambda i: (0, 0)),
            pl.BlockSpec((step, depth), lambda i: (i, column)),
        ]
        + [pl.BlockSpec((count, step), lambda i: (0, i))] * (cores - 1),
        out_specs=[pl.BlockSpec((piece, step), lambda i: (0, i))] * team,
        out_shape=[jax.ShapeDtypeStruct((piece, width), bf16 if d else f32) for d in range(team)],
        cost_estimate=pl.CostEstimate(
            flops=2 * count * depth * width,
            bytes_accessed=2 * width * (depth + 2 * count),
            transcendentals=0,
        ),
    )(rows[0] if stack is None else stack, weight, *others)
    got = [swap(out[d], "t", d) for d in range(1, team)]
    value = out[0]
    for v in got:
        value = value + v.astype(f32)
    return value, out


def grads_kernel(counts, *refs):
    out_ref = refs[-1]
    place = column = 0
    for count in counts:
        total = None
        for k in range(place, place + count):
            value = dot(refs[2 * k][...], refs[2 * k + 1][...], 0, 0)
            total = value if total is None else total + value
        width = total.shape[1]
        out_ref[:, column : column + width] = total.astype(bf16)
        place, column = place + count, column + width


def grads(groups, rows, columns):
    width = groups[0][0][0].shape[1]
    step = min(512, width)
    specs, arrays = [], []
    for pieces in groups:
        for left, left_at, right, right_at in pieces:
            specs.append(pl.BlockSpec((rows, step), lambda i, at=left_at: (at, i)))
            specs.append(pl.BlockSpec((rows, columns), lambda i, at=right_at: (at, 0)))
            arrays += [left, right]
    wide = columns * len(groups)
    value = pl.pallas_call(
        partial(grads_kernel, [len(p) for p in groups]),
        grid=(width // step,),
        in_specs=specs,
        out_specs=pl.BlockSpec((step, wide), lambda i: (i, 0)),
        out_shape=jax.ShapeDtypeStruct((width, wide), bf16),
        cost_estimate=pl.CostEstimate(
            flops=rows * len(arrays) * width * columns,
            bytes_accessed=rows * len(arrays) * (width + columns),
            transcendentals=0,
        ),
    )(*arrays)
    return lax.psum_scatter(value, "g", scatter_dimension=0, tiled=True)


SUB = 128


def blocks_of(ref):
    size = min(SUB, ref.shape[0])
    return [slice(i, i + size) for i in range(0, ref.shape[0], size)]


def unit_kernel(hidden_ref, weight_ref, grad_ref, act_out, grad_out):
    for at in blocks_of(hidden_ref):
        value = dot(hidden_ref[at], weight_ref[...])
        cumulative = 0.5 + 0.5 * lax.erf(value * (0.5**0.5))
        density = jnp.exp(-0.5 * value * value) * 0.3989422804014327
        act_out[at] = (value * cumulative).astype(bf16)
        grad_out[at] = (grad_ref[at] * (cumulative + value * density)).astype(bf16)


def unit_step(hidden, weight, grad, units, h):
    rows, width = hidden.shape
    size = min(256, rows)
    own = lambda i: (i, 0)
    shape = jax.ShapeDtypeStruct((rows, units), bf16)
    return pl.pallas_call(
        unit_kernel,
        grid=(rows // size,),
        in_specs=[
            pl.BlockSpec((size, width), own),
            pl.BlockSpec((width, units), lambda i: (0, 0)),
            pl.BlockSpec((size, units), lambda i: (h * (rows // size) + i, 0)),
        ],
        out_specs=[pl.BlockSpec((size, units), own)] * 2,
        out_shape=[shape] * 2,
        cost_estimate=pl.CostEstimate(
            flops=2 * rows * width * units, bytes_accessed=2 * rows * width, transcendentals=0
        ),
    )(hidden, weight, grad)


def chosen(refs, at):
    team = at[1]
    value = refs[0][...]
    for e in range(1, len(refs)):
        value = jnp.where(at[0] >= e * team, refs[e][...], value)
    return value


def weights_of(rate, seg_col, seg_row):
    size = seg_col.shape[0]
    row = lax.broadcasted_iota(jnp.int32, (size, size), 0)
    col = lax.broadcasted_iota(jnp.int32, (size, size), 1)
    offset = row - col
    valid = (offset >= 0) & (seg_col == seg_row)
    decay = jnp.where(valid, jnp.exp(jnp.maximum(offset, 0).astype(f32) * rate), 0.0)
    place = lax.broadcasted_iota(jnp.int32, (size, 1), 0)
    ahead = jnp.exp((place + 1).astype(f32) * rate)
    behind = jnp.exp((size - 1 - place).astype(f32) * rate)
    return decay, ahead, behind


def forward_kernel(cores, team, order, firsts, lasts, before_group, floats, *refs):
    qkv_refs = refs[:cores]
    col_ref, row_ref, start_ref, normed_ref, scale_ref, states_ref, state = refs[cores:]
    step = pl.program_id(0)
    rank = step
    at = order[rank]
    rate = floats[0]

    @pl.when(step == 0)
    def _():
        state[...] = start_ref[...].astype(f32)

    qkv = chosen(qkv_refs, (at, team))
    query, key, value = qkv[:, :KEY], qkv[:, KEY : 2 * KEY], qkv[:, 2 * KEY :]
    seg = col_ref[...]
    grown = jnp.exp(jnp.full((1, 1), 1.0, f32) * floats[1])
    decay, ahead, behind = weights_of(rate, seg, row_ref[0])
    first, last = firsts[at], lasts[at]
    before = jnp.where(rank == 0, before_group[0], lasts[order[jnp.maximum(rank - 1, 0)]])
    ahead = jnp.where((seg == first) & (before == first), ahead, 0.0)
    behind = jnp.where(seg == last, behind, 0.0)
    carry = jnp.where((before == first) & (first == last), grown, 0.0)
    held = state[...].astype(bf16)
    states_ref[0] = held
    scores = dot(query, key, 1, 1)
    weights = (scores * decay).astype(bf16)
    mixed = dot(weights, value) + ahead * dot(query, held)
    scale = lax.rsqrt(jnp.mean(mixed * mixed, axis=-1, keepdims=True) + eps_group)
    normed_ref[...] = mixed * scale
    scale_ref[...] = scale
    state[...] = dot((key * behind).astype(bf16), value, 0, 0) + carry * state[...]


def backward_kernel(cores, team, order, firsts, lasts, before_group, floats, *refs):
    groups = [refs[i * cores : (i + 1) * cores] for i in range(4)]
    qkv_refs, mixed_refs, rest_refs, gate_refs = groups
    states_ref, col_ref, row_ref, start_ref, out_ref, state = refs[4 * cores :]
    step = pl.program_id(0)
    rank = pl.num_programs(0) - 1 - step
    at = order[rank]
    rate = floats[0]

    @pl.when(step == 0)
    def _():
        state[...] = start_ref[...].astype(f32)

    qkv = chosen(qkv_refs, (at, team))
    grad = chosen(mixed_refs, (at, team))
    query, key, value = qkv[:, :KEY], qkv[:, KEY : 2 * KEY], qkv[:, 2 * KEY :]
    seg = col_ref[...]
    grown = jnp.exp(jnp.full((1, 1), 1.0, f32) * floats[1])
    decay, ahead, behind = weights_of(rate, seg, row_ref[0])
    first, last = firsts[at], lasts[at]
    before = jnp.where(rank == 0, before_group[0], lasts[order[jnp.maximum(rank - 1, 0)]])
    ahead = jnp.where((seg == first) & (before == first), ahead, 0.0)
    behind = jnp.where(seg == last, behind, 0.0)
    carry = jnp.where((before == first) & (first == last), grown, 0.0)
    held = state[...].astype(bf16)
    weights = (dot(query, key, 1, 1) * decay).astype(bf16)
    grad_rest = chosen(rest_refs, (at, team))
    grad_weights = dot(grad, value, 1, 1) + dot(grad_rest, value, 1, 1)
    grad_scores = (grad_weights * decay).astype(bf16)
    grad_query = dot(grad_scores, key) + ahead * dot(grad, states_ref[0], 1, 1)
    grad_key = dot(grad_scores, query, 0, 0) + behind * dot(value, held, 1, 1)
    grad_value = dot(weights, grad, 0, 0) + behind * dot(key, held)
    out_ref[:, :KEY] = grad_query.astype(bf16)
    out_ref[:, KEY : 2 * KEY] = grad_key.astype(bf16)
    out_ref[:, 2 * KEY : 2 * KEY + VALUE] = grad_value.astype(bf16)
    out_ref[:, 2 * KEY + VALUE :] = chosen(gate_refs, (at, team))
    state[...] = dot((query * ahead).astype(bf16), grad, 0, 0) + carry * state[...]


def walk(kernel, cores, team, edges, split, whole, outs, reverse, flops, moved):
    chunks = cores * team

    def at(step, order):
        return order[chunks - 1 - step] if reverse else order[step]

    def block(e, width, size):
        return pl.BlockSpec(
            (size, width),
            lambda i, order, *_: (jnp.clip(at(i, order) - e * team, 0, team - 1), 0),
        )

    def spec(shape, each):
        zeros = (0,) * (len(shape) - 1)
        if each:
            return pl.BlockSpec(shape, lambda i, order, *_: (at(i, order),) + zeros)
        return pl.BlockSpec(shape, lambda i, order, *_: (0,) + zeros)

    arrays, specs = [], []
    for group in split:
        for e, array in enumerate(group):
            arrays.append(array)
            specs.append(block(e, array.shape[1], array.shape[0] // team))
    for array, shape, each in whole:
        arrays.append(array)
        specs.append(spec(shape, each))
    return pl.pallas_call(
        partial(kernel, cores, team),
        grid_spec=pltpu.PrefetchScalarGridSpec(
            num_scalar_prefetch=len(edges),
            grid=(chunks,),
            in_specs=specs,
            out_specs=[spec(shape, each) for _, shape, each in outs],
            scratch_shapes=[pltpu.VMEM((KEY, VALUE), f32)],
        ),
        out_shape=[shape for shape, _, _ in outs],
        cost_estimate=pl.CostEstimate(flops=flops, bytes_accessed=moved, transcendentals=0),
    )(*edges, *arrays)


def gate_back_kernel(*refs):
    grad_refs = refs[:2]
    weight_ref, gate_ref, normed_ref, scale_ref, gate_out, mixed_out, rest_out = refs[2:]
    half = grad_refs[0].shape[0]
    for h in range(2):
        at = slice(h * half, (h + 1) * half)
        grad_gated = dot(grad_refs[h][...], weight_ref[...])
        gate = gate_ref[at]
        normed = normed_ref[at]
        sigmoid = 1.0 / (1.0 + jnp.exp(-gate))
        gate_out[at] = (
            grad_gated * normed * (sigmoid + gate * sigmoid * (1.0 - sigmoid))
        ).astype(bf16)
        grad_normed = grad_gated * (gate * sigmoid)
        along = jnp.mean(grad_normed * normed, axis=-1, keepdims=True)
        grad_mixed = scale_ref[at] * (grad_normed - normed * along)
        rounded = grad_mixed.astype(bf16)
        mixed_out[at] = rounded
        rest_out[at] = (grad_mixed - rounded.astype(f32)).astype(bf16)


def gate_back(grads, weight, gate, normed, scale, e, team):
    rows, width = 2 * grads[0].shape[0], grads[0].shape[1]
    size = rows // team
    own = lambda d: (d, 0)
    far = lambda d: (e * team + d, 0)
    shape = jax.ShapeDtypeStruct((rows, VALUE), bf16)
    return pl.pallas_call(
        gate_back_kernel,
        grid=(team,),
        in_specs=[
            pl.BlockSpec((size // 2, width), own),
            pl.BlockSpec((size // 2, width), own),
            pl.BlockSpec(weight.shape, lambda d: (0, 0)),
            pl.BlockSpec((size, VALUE), own),
            pl.BlockSpec((size, VALUE), far),
            pl.BlockSpec((size, 1), far),
        ],
        out_specs=[pl.BlockSpec((size, VALUE), own)] * 3,
        out_shape=[shape] * 3,
        cost_estimate=pl.CostEstimate(
            flops=2 * rows * width * VALUE, bytes_accessed=2 * rows * width, transcendentals=0
        ),
    )(*grads, weight, gate, normed, scale)


def shards(tokens, norm_gains, w_mixer, w_out, w_up, w_down, seg_ids, cotangent):
    team, _, cores = (lax.axis_size(a) for a in ("t", "g", "h"))
    _, j, c = (lax.axis_index(a) for a in ("g", "t", "h"))
    heads_here = w_mixer.shape[2]
    length, _ = tokens.shape
    size = length // cores
    chunks = team
    near = range(cores)
    units = w_up.shape[2] // team

    rows_here = w_mixer.shape[1]
    mixer_slabs = w_mixer[0].transpose(1, 0, 2)
    rest = jnp.concatenate(
        [
            w_out[0].reshape(team, VALUE, rows_here).transpose(0, 2, 1),
            w_up[0].reshape(rows_here, team, units).transpose(1, 0, 2),
            w_down[0].reshape(team, units, rows_here).transpose(0, 2, 1),
        ],
        axis=2,
    )
    mixer_rows = join(deal(lambda m: lax.dynamic_index_in_dim(mixer_slabs, m, 0, keepdims=False)))
    whole = partial(lax.all_gather, axis_name="g", axis=0, tiled=True)
    w_mixer_all = whole(mixer_rows)

    segs = [seg_ids] + [swap(seg_ids, "t", d) for d in range(1, team)]
    seg = jnp.stack(
        [
            lax.dynamic_slice_in_dim(segs[d], (c ^ e) * size, size, 0)
            for e in near
            for d in range(team)
        ]
    )
    chunks = cores * team
    rank = jnp.arange(chunks)
    order = (((rank % cores) ^ c) * team + ((rank // cores) ^ j)).astype(jnp.int32)
    place = jnp.stack([(j ^ d) * length + (c ^ e) * size for e in near for d in range(team)])
    group_length = team * length
    group_first = jnp.min(seg, keepdims=True)
    group_last = jnp.max(seg, keepdims=True)
    before_group = shift(group_last + 1, 1) - 1
    head = c * heads_here + j
    rate = jnp.log1p(-jnp.exp2(-5.0 - head.astype(f32)))
    floats = rate * jnp.array([1.0, size], f32)
    seg_col = seg.reshape(-1, 1)
    seg_row = seg[:, None, :]
    token = (place[:, None] + jnp.arange(size)).reshape(-1, 1)
    to_end = jnp.where(
        seg_col == group_last, jnp.exp((group_length - 1 - token).astype(f32) * rate), 0.0
    )
    from_start = jnp.where(
        seg_col == before_group, jnp.exp((token + 1).astype(f32) * rate), 0.0
    )
    through = jnp.where(
        (before_group == group_first) & (group_first == group_last),
        jnp.exp(group_length * rate),
        0.0,
    )
    edges = (order, seg[:, 0], seg[:, size - 1], before_group.reshape(1), floats)
    hops = -(-(SEQ_MOST - 1) // group_length)
    rows = team * size

    def here(value, e):
        return value[e * rows : (e + 1) * rows]

    def state_sum(left, factor, right):
        return sum(
            dot((left[e] * here(factor, e)).astype(bf16), right[e], 0, 0) for e in near
        )

    def passed(value, steps):
        state = shift(value.astype(bf16), steps)
        for _ in range(hops - 1):
            state = shift((value + through * state.astype(f32)).astype(bf16), steps)
        return state

    gain_one, gain_two = norm_gains[0, 0], norm_gains[0, 1]
    stream = lax.dynamic_slice_in_dim(tokens, c * size, size, 0).astype(f32)
    cot = lax.dynamic_slice_in_dim(cotangent, c * size, size, 0)
    hidden_own, normed1, scaled1 = layer_norm(stream, gain_one)
    hidden = share(after(hidden_own.astype(bf16), mixer_rows))
    rest = after(rest, mixer_rows)
    rest_rows = join(deal(lambda m: lax.dynamic_index_in_dim(rest, m, 0, keepdims=False)))
    w_o = whole(rest_rows[:, :VALUE])
    w_ud = whole(rest_rows[:, VALUE:])
    cot_all = share(after(cot, hidden[0]), True)

    qkv = [dot(h, w_mixer_all[:, : 2 * KEY + VALUE]).astype(bf16) for h in hidden]
    end_state = state_sum(
        [v[:, KEY : 2 * KEY] for v in qkv], to_end, [v[:, 2 * KEY :] for v in qkv]
    )
    chunk_flops = 2 * size * size * (KEY + VALUE) + 4 * size * KEY * VALUE
    state_in = passed(end_state, 1)
    normed, scale, states = walk(
        forward_kernel,
        cores,
        team,
        edges,
        [qkv],
        [
            (seg_col, (size, 1), True),
            (seg_row, (1, 1, size), True),
            (state_in, (KEY, VALUE), False),
        ],
        [
            (jax.ShapeDtypeStruct((chunks * size, VALUE), f32), (size, VALUE), True),
            (jax.ShapeDtypeStruct((chunks * size, 1), f32), (size, 1), True),
            (jax.ShapeDtypeStruct((chunks, KEY, VALUE), bf16), (1, KEY, VALUE), True),
        ],
        False,
        chunks * chunk_flops,
        chunks * size * 4096,
    )
    gate = [dot(h, w_mixer_all[:, 2 * KEY + VALUE :]) for h in hidden]
    gate = after(gate, state_in)
    gated = []
    for e in near:
        gated.append(
            (gate[e] * jax.nn.sigmoid(gate[e]) * here(normed, e)).astype(bf16)
        )
    half = size // 2
    both = range(2)

    def of_half(value, h):
        return value[h * half : (h + 1) * half]

    gated_half = [
        [v.reshape(team, 2, half, VALUE)[:, h].reshape(-1, VALUE) for h in both] for v in gated
    ]
    grad_act = [dot(t, w_ud[:, units:]) for t in cot_all]
    own = None
    streams, normed2, scaled2, hidden2, act, grad_up = [], [], [], [], [], []
    for h in both:
        added = reduce_half(gated, half, h, w_o, 0, own)[0]
        streams.append(of_half(stream, h) + added)
        own, n, s = layer_norm(streams[h], gain_two)
        normed2.append(n)
        scaled2.append(s)
        own = own.astype(bf16)
        hidden2.append(share(own))
        pairs = []
        for e in near:
            pairs.append(unit_step(hidden2[h][e], w_ud, grad_act[e], units, h))
        act.append([p[0] for p in pairs])
        grad_up.append([p[1] for p in pairs])

    def both_cores(rows):
        rows = rows.astype(bf16)
        got = [rows] + [swap(rows, "h", e) for e in range(1, cores)]
        return join(straight(got, "h"))

    grad, grad_all, gain_grad_two = [], [], 0.0
    for h in both:
        value, sent = reduce_half(grad_up[h], half, h, w_ud, 0, own)
        norm_part, gain_part = norm_back(value, normed2[h], scaled2[h], gain_two)
        gain_grad_two = gain_grad_two + gain_part
        grad.append(of_half(cot, h).astype(f32) + norm_part)
        own = grad[h].astype(bf16)
        grad_all.append(share(own))
    cot_late, hidden_late = after((cot_all, hidden2), sent)
    halves = [(e, h) for e in near for h in both]
    part = team * half
    units_done = grads(
        [
            [(hidden_late[h][e], 0, grad_up[h][e], 0) for e, h in halves],
            [(cot_late[e], h, act[h][e], 0) for e, h in halves],
        ],
        part,
        units,
    )
    backs = []
    for e in near:
        grad_here = [grad_all[h][e] for h in both]
        backs.append(gate_back(grad_here, w_o, gate[e], normed, scale, e, team))
    grad_gate, grad_mixed, mixed_rest = ([v[i] for v in backs] for i in range(3))
    heads_done = grads(
        [
            [(grad_all[h][e], 0, gated_half[e][h], 0) for e, h in halves],
            [(hidden[e], h, grad_gate[e], h) for e, h in halves],
        ],
        part,
        VALUE,
    )
    grad_before = state_sum([v[:, :KEY] for v in qkv], from_start, grad_mixed)
    grad_in = passed(grad_before, -1)
    act_rows = [jnp.concatenate([act[h][e] for h in both], axis=0) for e in near]
    added = reduce(after(act_rows, grad_before), w_ud, 1, halves=2)[0]
    (proj,) = walk(
        backward_kernel,
        cores,
        team,
        edges,
        [qkv, grad_mixed, mixed_rest, grad_gate],
        [
            (states, (1, KEY, VALUE), True),
            (seg_col, (size, 1), True),
            (seg_row, (1, 1, size), True),
            (grad_in, (KEY, VALUE), False),
        ],
        [
            (
                jax.ShapeDtypeStruct((chunks * size, 2 * KEY + 2 * VALUE), bf16),
                (size, 2 * KEY + 2 * VALUE),
                True,
            ),
        ],
        True,
        3 * chunks * chunk_flops,
        chunks * size * 12000,
    )
    grad_proj = [here(proj, e) for e in near]
    qkv_done = grads([[(hidden[e], 0, proj, e) for e in near]], rows, 2 * KEY + VALUE)
    grad_hidden = reduce(grad_proj, w_mixer_all, 0, proj)[0]
    output = both_cores(jnp.concatenate(streams, axis=0) + added)
    norm_part, gain_grad_one = norm_back(grad_hidden, normed1, scaled1, gain_one)
    input_grad = both_cores(jnp.concatenate(grad, axis=0) + norm_part)
    gain_grad = total(jnp.stack([gain_grad_one, gain_grad_two]))

    def own_rows(done):
        return deal(lambda m: lax.dynamic_slice_in_dim(done, m * rows_here, rows_here, 0))

    own_units = own_rows(units_done)
    own_heads = own_rows(heads_done)
    own_heads = after(own_heads, gain_grad_one)
    own_qkv = own_rows(qkv_done)
    mixer_grad = jnp.concatenate(
        [
            jnp.stack(own_qkv, axis=1),
            jnp.stack([v[:, VALUE:] for v in own_heads], axis=1),
        ],
        axis=-1,
    ).astype(f32)
    up_grad = jnp.concatenate([v[:, :units] for v in own_units], axis=1).astype(f32)
    down_grad = jnp.concatenate([v[:, units:].T for v in own_units], axis=0).astype(f32)
    out_grad = jnp.concatenate([v[:, :VALUE].T for v in own_heads], axis=0).astype(f32)
    return (
        output,
        input_grad,
        gain_grad[None],
        mixer_grad[None],
        out_grad[None],
        up_grad[None],
        down_grad[None],
    )


def solution(mesh):
    devices, cores = mesh.devices.shape
    team = team_size(devices, HEADS // cores)
    fine = Mesh(mesh.devices.reshape(devices // team, team, cores), ("g", "t", "h"))
    fsdp = ("g", "t")

    return jax.shard_map(
        shards,
        mesh=fine,
        in_specs=(
            P(fsdp, None),
            P(),
            P(None, fsdp, "h", None),
            P(None, "h", fsdp),
            P(None, fsdp, "h"),
            P(None, "h", fsdp),
            P(fsdp),
            P(fsdp, None),
        ),
        out_specs=(
            P(fsdp, None),
            P(fsdp, None),
            P(),
            P(None, fsdp, "h", None),
            P(None, "h", fsdp),
            P(None, fsdp, "h"),
            P(None, "h", fsdp),
        ),
        check_vma=False,
    )
```

```python
from functools import partial

import jax
import jax.numpy as jnp
from jax import lax
from jax.experimental import pallas as pl
from jax.experimental.pallas import tpu as pltpu
from jax.sharding import Mesh, PartitionSpec as P


HEADS = 8
KEY = 256
VALUE = 512
SEQ_MOST = 2048

eps_norm = 1e-05
eps_group = 1e-06
bf16 = jnp.bfloat16
f32 = jnp.float32


def team_size(devices, heads_here):
    team = 4
    while heads_here % team or devices % team:
        team //= 2
    return team


def dot(a, b, left=1, right=0):
    return lax.dot_general(a, b, (((left,), (right,)), ((), ())), preferred_element_type=f32)


def layer_norm(stream, gain):
    centered = stream - jnp.mean(stream, axis=-1, keepdims=True)
    scaled = lax.rsqrt(jnp.mean(centered * centered, axis=-1, keepdims=True) + eps_norm)
    normed = centered * scaled
    return (normed * gain, normed, scaled)


def norm_back(grad_out, normed, scaled, gain):
    grad_norm = grad_out * gain
    inner = jnp.mean(grad_norm, axis=-1, keepdims=True)
    along = jnp.mean(grad_norm * normed, axis=-1, keepdims=True)
    return (scaled * (grad_norm - inner - normed * along), jnp.sum(grad_out * normed, axis=0))


def swap(value, axis, d):
    count = lax.axis_size(axis)
    return lax.ppermute(value, axis, [(i, i ^ d) for i in range(count)])


def shift(value, steps):
    count = lax.axis_size("g")
    pairs = [(i, i + steps) for i in range(count) if 0 <= i + steps < count]
    return lax.ppermute(value, "g", pairs)


def total(value):
    for axis in ("h", "t", "g"):
        parts = [value] + [swap(value, axis, d) for d in range(1, lax.axis_size(axis))]
        while len(parts) > 1:
            parts = [parts[k] + parts[k + 1] for k in range(0, len(parts), 2)]
        value = parts[0]
    return value


def straight(pieces, axis):
    mine = lax.axis_index(axis)
    pieces = list(pieces)
    bit = 1
    while bit < len(pieces):
        odd = (mine & bit) != 0
        pieces = [jnp.where(odd, pieces[i ^ bit], pieces[i]) for i in range(len(pieces))]
        bit *= 2
    return pieces


def deal(pick):
    mine = lax.axis_index("t")
    got = [pick(mine)]
    for d in range(1, lax.axis_size("t")):
        got.append(swap(pick(mine ^ d), "t", d))
    return straight(got, "t")


def join(parts):
    rows = parts[0].shape[0]
    out = jnp.zeros((rows * len(parts),) + parts[0].shape[1:], parts[0].dtype)
    for i, part in enumerate(parts):
        out = lax.dynamic_update_slice_in_dim(out, part, i * rows, 0)
    return out


def share(own, halves=False, relay=False):
    team = lax.axis_size("t")
    relay = relay and team == 4
    parts = [own] + [swap(own, "t", d) for d in range(1, 3 if relay else team)]
    if relay:
        half = own.shape[1] // 2
        left = swap(parts[1][:, :half], "t", 2)
        right = swap(parts[2][:, half:], "t", 1)
        count = own.shape[0]
        rows = jnp.zeros((team * count, own.shape[1]), own.dtype)
        for d, part in enumerate(parts):
            rows = lax.dynamic_update_slice(rows, part, (d * count, 0))
        rows = lax.dynamic_update_slice(rows, left, (3 * count, 0))
        rows = lax.dynamic_update_slice(rows, right, (3 * count, half))
        return [rows] + [swap(rows, "h", e) for e in range(1, lax.axis_size("h"))]
    if halves:
        half = own.shape[0] // 2
        parts = [p[h * half : (h + 1) * half] for h in range(2) for p in parts]
    rows = join(parts)
    return [rows] + [swap(rows, "h", e) for e in range(1, lax.axis_size("h"))]


def after(values, first):
    return lax.optimization_barrier((values, first))[0]


def reduce_kernel(team, halves, rows_ref, weight_ref, *refs):
    others, outs = refs[: len(refs) - team], refs[len(refs) - team :]
    rows = rows_ref[...]
    total = dot(rows.reshape(-1, rows.shape[-1]), weight_ref[...], 1, 1)
    for other in others:
        total = total + other[...].astype(f32)
    piece = total.shape[0] // (team * halves)
    for d, out in enumerate(outs):
        for h in range(halves):
            at = (h * team + d) * piece
            out[h * piece : (h + 1) * piece] = total[at : at + piece].astype(out.dtype)


def other_kernel(rows_ref, weight_ref, out_ref):
    rows = rows_ref[...]
    out_ref[...] = dot(rows.reshape(-1, rows.shape[-1]), weight_ref[...], 1, 1).astype(bf16)


def reduce_half(rows, half, h, weight, column, first=None):
    team, cores = lax.axis_size("t"), len(rows)
    width = weight.shape[0]
    step = min(1024, width)

    def spec(value):
        depth = value.shape[-1]
        full = value.shape[0] != team * half
        value = value.reshape(team, -1, depth)
        return value, pl.BlockSpec((team, half, depth), lambda i: (0, h if full else 0, 0))

    def call(kernel, e, others, shapes):
        value, own = spec(rows[e])
        depth = value.shape[-1]
        return pl.pallas_call(
            kernel,
            grid=(width // step,),
            in_specs=[own, pl.BlockSpec((step, depth), lambda i: (i, column))]
            + [pl.BlockSpec((count, step), lambda i: (0, i)) for _ in others],
            out_specs=[pl.BlockSpec((s.shape[0], step), lambda i: (0, i)) for s in shapes],
            out_shape=shapes,
            cost_estimate=pl.CostEstimate(
                flops=2 * count * depth * width,
                bytes_accessed=2 * width * (depth + count),
                transcendentals=0,
            ),
        )(value, weight, *others)

    count = team * half
    shape = [jax.ShapeDtypeStruct((count, width), bf16)]
    mine = [call(other_kernel, e, [], shape)[0] for e in range(1, cores)]
    others = [swap(v, "h", e) for e, v in enumerate(mine, 1)]
    shapes = [jax.ShapeDtypeStruct((count // team, width), bf16 if d else f32) for d in range(team)]
    out = call(partial(reduce_kernel, team, 1), 0, others, shapes)
    got = [swap(out[d], "t", d) for d in range(1, team)]
    if first is not None:
        got = after(got, first)
    value = out[0]
    for v in got:
        value = value + v.astype(f32)
    return value, out


def reduce(rows, weight, column, stack=None, halves=1):
    team, cores = lax.axis_size("t"), len(rows)
    count, depth = rows[0].shape
    width = weight.shape[0]
    step = min(1024 if depth <= 512 else 512, width)
    part = weight[:, column * depth : (column + 1) * depth]
    first = [dot(rows[e], part, 1, 1).astype(bf16) for e in range(1, cores)]
    others = [swap(v, "h", e) for e, v in enumerate(first, 1)]
    piece = count // team
    out = pl.pallas_call(
        partial(reduce_kernel, team, halves),
        grid=(width // step,),
        in_specs=[
            pl.BlockSpec((count, depth), lambda i: (0, 0)),
            pl.BlockSpec((step, depth), lambda i: (i, column)),
        ]
        + [pl.BlockSpec((count, step), lambda i: (0, i))] * (cores - 1),
        out_specs=[pl.BlockSpec((piece, step), lambda i: (0, i))] * team,
        out_shape=[jax.ShapeDtypeStruct((piece, width), bf16 if d else f32) for d in range(team)],
        cost_estimate=pl.CostEstimate(
            flops=2 * count * depth * width,
            bytes_accessed=2 * width * (depth + 2 * count),
            transcendentals=0,
        ),
    )(rows[0] if stack is None else stack, weight, *others)
    got = [swap(out[d], "t", d) for d in range(1, team)]
    value = out[0]
    for v in got:
        value = value + v.astype(f32)
    return value, out


def grads_kernel(counts, *refs):
    out_ref = refs[-1]
    place = column = 0
    for count in counts:
        total = None
        for k in range(place, place + count):
            value = dot(refs[2 * k][...], refs[2 * k + 1][...], 0, 0)
            total = value if total is None else total + value
        width = total.shape[1]
        out_ref[:, column : column + width] = total.astype(bf16)
        place, column = place + count, column + width


def grads(groups, rows, columns):
    width = groups[0][0][0].shape[1]
    step = min(512, width)
    specs, arrays = [], []
    for pieces in groups:
        for left, left_at, right, right_at in pieces:
            specs.append(pl.BlockSpec((rows, step), lambda i, at=left_at: (at, i)))
            specs.append(pl.BlockSpec((rows, columns), lambda i, at=right_at: (at, 0)))
            arrays += [left, right]
    wide = columns * len(groups)
    value = pl.pallas_call(
        partial(grads_kernel, [len(p) for p in groups]),
        grid=(width // step,),
        in_specs=specs,
        out_specs=pl.BlockSpec((step, wide), lambda i: (i, 0)),
        out_shape=jax.ShapeDtypeStruct((width, wide), bf16),
        cost_estimate=pl.CostEstimate(
            flops=rows * len(arrays) * width * columns,
            bytes_accessed=rows * len(arrays) * (width + columns),
            transcendentals=0,
        ),
    )(*arrays)
    return lax.psum_scatter(value, "g", scatter_dimension=0, tiled=True)


SUB = 128


def blocks_of(ref):
    size = min(SUB, ref.shape[0])
    return [slice(i, i + size) for i in range(0, ref.shape[0], size)]


def unit_kernel(hidden_ref, weight_ref, grad_ref, act_out, grad_out):
    for at in blocks_of(hidden_ref):
        value = dot(hidden_ref[at], weight_ref[...])
        cumulative = 0.5 + 0.5 * lax.erf(value * (0.5**0.5))
        density = jnp.exp(-0.5 * value * value) * 0.3989422804014327
        act_out[at] = (value * cumulative).astype(bf16)
        grad_out[at] = (grad_ref[at] * (cumulative + value * density)).astype(bf16)


def unit_step(hidden, weight, grad, units, h):
    rows, width = hidden.shape
    size = min(256, rows)
    own = lambda i: (i, 0)
    shape = jax.ShapeDtypeStruct((rows, units), bf16)
    return pl.pallas_call(
        unit_kernel,
        grid=(rows // size,),
        in_specs=[
            pl.BlockSpec((size, width), own),
            pl.BlockSpec((width, units), lambda i: (0, 0)),
            pl.BlockSpec((size, units), lambda i: (h * (rows // size) + i, 0)),
        ],
        out_specs=[pl.BlockSpec((size, units), own)] * 2,
        out_shape=[shape] * 2,
        cost_estimate=pl.CostEstimate(
            flops=2 * rows * width * units, bytes_accessed=2 * rows * width, transcendentals=0
        ),
    )(hidden, weight, grad)


def chosen(refs, at):
    team = at[1]
    value = refs[0][...]
    for e in range(1, len(refs)):
        value = jnp.where(at[0] >= e * team, refs[e][...], value)
    return value


def weights_of(rate, seg_col, seg_row):
    size = seg_col.shape[0]
    row = lax.broadcasted_iota(jnp.int32, (size, size), 0)
    col = lax.broadcasted_iota(jnp.int32, (size, size), 1)
    offset = row - col
    valid = (offset >= 0) & (seg_col == seg_row)
    decay = jnp.where(valid, jnp.exp(jnp.maximum(offset, 0).astype(f32) * rate), 0.0)
    place = lax.broadcasted_iota(jnp.int32, (size, 1), 0)
    ahead = jnp.exp((place + 1).astype(f32) * rate)
    behind = jnp.exp((size - 1 - place).astype(f32) * rate)
    return decay, ahead, behind


def forward_kernel(cores, team, order, firsts, lasts, before_group, floats, *refs):
    qkv_refs = refs[:cores]
    col_ref, row_ref, start_ref, normed_ref, scale_ref, states_ref, state = refs[cores:]
    step = pl.program_id(0)
    rank = step
    at = order[rank]
    rate = floats[0]

    @pl.when(step == 0)
    def _():
        state[...] = start_ref[...].astype(f32)

    qkv = chosen(qkv_refs, (at, team))
    query, key, value = qkv[:, :KEY], qkv[:, KEY : 2 * KEY], qkv[:, 2 * KEY :]
    seg = col_ref[...]
    grown = jnp.exp(jnp.full((1, 1), 1.0, f32) * floats[1])
    decay, ahead, behind = weights_of(rate, seg, row_ref[0])
    first, last = firsts[at], lasts[at]
    before = jnp.where(rank == 0, before_group[0], lasts[order[jnp.maximum(rank - 1, 0)]])
    ahead = jnp.where((seg == first) & (before == first), ahead, 0.0)
    behind = jnp.where(seg == last, behind, 0.0)
    carry = jnp.where((before == first) & (first == last), grown, 0.0)
    held = state[...].astype(bf16)
    states_ref[0] = held
    scores = dot(query, key, 1, 1)
    weights = (scores * decay).astype(bf16)
    mixed = dot(weights, value) + ahead * dot(query, held)
    scale = lax.rsqrt(jnp.mean(mixed * mixed, axis=-1, keepdims=True) + eps_group)
    normed_ref[...] = mixed * scale
    scale_ref[...] = scale
    state[...] = dot((key * behind).astype(bf16), value, 0, 0) + carry * state[...]


def backward_kernel(cores, team, order, firsts, lasts, before_group, floats, *refs):
    groups = [refs[i * cores : (i + 1) * cores] for i in range(4)]
    qkv_refs, mixed_refs, rest_refs, gate_refs = groups
    states_ref, col_ref, row_ref, start_ref, out_ref, state = refs[4 * cores :]
    step = pl.program_id(0)
    rank = pl.num_programs(0) - 1 - step
    at = order[rank]
    rate = floats[0]

    @pl.when(step == 0)
    def _():
        state[...] = start_ref[...].astype(f32)

    qkv = chosen(qkv_refs, (at, team))
    grad = chosen(mixed_refs, (at, team))
    query, key, value = qkv[:, :KEY], qkv[:, KEY : 2 * KEY], qkv[:, 2 * KEY :]
    seg = col_ref[...]
    grown = jnp.exp(jnp.full((1, 1), 1.0, f32) * floats[1])
    decay, ahead, behind = weights_of(rate, seg, row_ref[0])
    first, last = firsts[at], lasts[at]
    before = jnp.where(rank == 0, before_group[0], lasts[order[jnp.maximum(rank - 1, 0)]])
    ahead = jnp.where((seg == first) & (before == first), ahead, 0.0)
    behind = jnp.where(seg == last, behind, 0.0)
    carry = jnp.where((before == first) & (first == last), grown, 0.0)
    held = state[...].astype(bf16)
    weights = (dot(query, key, 1, 1) * decay).astype(bf16)
    grad_rest = chosen(rest_refs, (at, team))
    grad_weights = dot(grad, value, 1, 1) + dot(grad_rest, value, 1, 1)
    grad_scores = (grad_weights * decay).astype(bf16)
    grad_query = dot(grad_scores, key) + ahead * dot(grad, states_ref[0], 1, 1)
    grad_key = dot(grad_scores, query, 0, 0) + behind * dot(value, held, 1, 1)
    grad_value = dot(weights, grad, 0, 0) + behind * dot(key, held)
    out_ref[:, :KEY] = grad_query.astype(bf16)
    out_ref[:, KEY : 2 * KEY] = grad_key.astype(bf16)
    out_ref[:, 2 * KEY : 2 * KEY + VALUE] = grad_value.astype(bf16)
    out_ref[:, 2 * KEY + VALUE :] = chosen(gate_refs, (at, team))
    state[...] = dot((query * ahead).astype(bf16), grad, 0, 0) + carry * state[...]


def walk(kernel, cores, team, edges, split, whole, outs, reverse, flops, moved):
    chunks = cores * team

    def at(step, order):
        return order[chunks - 1 - step] if reverse else order[step]

    def block(e, width, size):
        return pl.BlockSpec(
            (size, width),
            lambda i, order, *_: (jnp.clip(at(i, order) - e * team, 0, team - 1), 0),
        )

    def spec(shape, each):
        zeros = (0,) * (len(shape) - 1)
        if each:
            return pl.BlockSpec(shape, lambda i, order, *_: (at(i, order),) + zeros)
        return pl.BlockSpec(shape, lambda i, order, *_: (0,) + zeros)

    arrays, specs = [], []
    for group in split:
        for e, array in enumerate(group):
            arrays.append(array)
            specs.append(block(e, array.shape[1], array.shape[0] // team))
    for array, shape, each in whole:
        arrays.append(array)
        specs.append(spec(shape, each))
    return pl.pallas_call(
        partial(kernel, cores, team),
        grid_spec=pltpu.PrefetchScalarGridSpec(
            num_scalar_prefetch=len(edges),
            grid=(chunks,),
            in_specs=specs,
            out_specs=[spec(shape, each) for _, shape, each in outs],
            scratch_shapes=[pltpu.VMEM((KEY, VALUE), f32)],
        ),
        out_shape=[shape for shape, _, _ in outs],
        cost_estimate=pl.CostEstimate(flops=flops, bytes_accessed=moved, transcendentals=0),
    )(*edges, *arrays)


def gate_back_kernel(*refs):
    grad_refs = refs[:2]
    weight_ref, gate_ref, normed_ref, scale_ref, gate_out, mixed_out, rest_out = refs[2:]
    half = grad_refs[0].shape[0]
    for h in range(2):
        at = slice(h * half, (h + 1) * half)
        grad_gated = dot(grad_refs[h][...], weight_ref[...])
        gate = gate_ref[at]
        normed = normed_ref[at]
        sigmoid = 1.0 / (1.0 + jnp.exp(-gate))
        gate_out[at] = (
            grad_gated * normed * (sigmoid + gate * sigmoid * (1.0 - sigmoid))
        ).astype(bf16)
        grad_normed = grad_gated * (gate * sigmoid)
        along = jnp.mean(grad_normed * normed, axis=-1, keepdims=True)
        grad_mixed = scale_ref[at] * (grad_normed - normed * along)
        rounded = grad_mixed.astype(bf16)
        mixed_out[at] = rounded
        rest_out[at] = (grad_mixed - rounded.astype(f32)).astype(bf16)


def gate_back(grads, weight, gate, normed, scale, e, team):
    rows, width = 2 * grads[0].shape[0], grads[0].shape[1]
    size = rows // team
    own = lambda d: (d, 0)
    far = lambda d: (e * team + d, 0)
    shape = jax.ShapeDtypeStruct((rows, VALUE), bf16)
    return pl.pallas_call(
        gate_back_kernel,
        grid=(team,),
        in_specs=[
            pl.BlockSpec((size // 2, width), own),
            pl.BlockSpec((size // 2, width), own),
            pl.BlockSpec(weight.shape, lambda d: (0, 0)),
            pl.BlockSpec((size, VALUE), own),
            pl.BlockSpec((size, VALUE), far),
            pl.BlockSpec((size, 1), far),
        ],
        out_specs=[pl.BlockSpec((size, VALUE), own)] * 3,
        out_shape=[shape] * 3,
        cost_estimate=pl.CostEstimate(
            flops=2 * rows * width * VALUE, bytes_accessed=2 * rows * width, transcendentals=0
        ),
    )(*grads, weight, gate, normed, scale)


def shards(tokens, norm_gains, w_mixer, w_out, w_up, w_down, seg_ids, cotangent):
    team, _, cores = (lax.axis_size(a) for a in ("t", "g", "h"))
    _, j, c = (lax.axis_index(a) for a in ("g", "t", "h"))
    heads_here = w_mixer.shape[2]
    length, _ = tokens.shape
    size = length // cores
    chunks = team
    near = range(cores)
    units = w_up.shape[2] // team

    rows_here = w_mixer.shape[1]
    mixer_slabs = w_mixer[0].transpose(1, 0, 2)
    rest = jnp.concatenate(
        [
            w_out[0].reshape(team, VALUE, rows_here).transpose(0, 2, 1),
            w_up[0].reshape(rows_here, team, units).transpose(1, 0, 2),
            w_down[0].reshape(team, units, rows_here).transpose(0, 2, 1),
        ],
        axis=2,
    )
    mixer_rows = join(deal(lambda m: lax.dynamic_index_in_dim(mixer_slabs, m, 0, keepdims=False)))
    whole = partial(lax.all_gather, axis_name="g", axis=0, tiled=True)
    w_mixer_all = whole(mixer_rows)

    segs = [seg_ids] + [swap(seg_ids, "t", d) for d in range(1, team)]
    seg = jnp.stack(
        [
            lax.dynamic_slice_in_dim(segs[d], (c ^ e) * size, size, 0)
            for e in near
            for d in range(team)
        ]
    )
    chunks = cores * team
    rank = jnp.arange(chunks)
    order = (((rank % cores) ^ c) * team + ((rank // cores) ^ j)).astype(jnp.int32)
    place = jnp.stack([(j ^ d) * length + (c ^ e) * size for e in near for d in range(team)])
    group_length = team * length
    group_first = jnp.min(seg, keepdims=True)
    group_last = jnp.max(seg, keepdims=True)
    before_group = shift(group_last + 1, 1) - 1
    head = c * heads_here + j
    rate = jnp.log1p(-jnp.exp2(-5.0 - head.astype(f32)))
    floats = rate * jnp.array([1.0, size], f32)
    seg_col = seg.reshape(-1, 1)
    seg_row = seg[:, None, :]
    token = (place[:, None] + jnp.arange(size)).reshape(-1, 1)
    to_end = jnp.where(
        seg_col == group_last, jnp.exp((group_length - 1 - token).astype(f32) * rate), 0.0
    )
    from_start = jnp.where(
        seg_col == before_group, jnp.exp((token + 1).astype(f32) * rate), 0.0
    )
    through = jnp.where(
        (before_group == group_first) & (group_first == group_last),
        jnp.exp(group_length * rate),
        0.0,
    )
    edges = (order, seg[:, 0], seg[:, size - 1], before_group.reshape(1), floats)
    hops = -(-(SEQ_MOST - 1) // group_length)
    rows = team * size

    def here(value, e):
        return value[e * rows : (e + 1) * rows]

    def state_sum(left, factor, right):
        return sum(
            dot((left[e] * here(factor, e)).astype(bf16), right[e], 0, 0) for e in near
        )

    def passed(value, steps):
        state = shift(value.astype(bf16), steps)
        for _ in range(hops - 1):
            state = shift((value + through * state.astype(f32)).astype(bf16), steps)
        return state

    gain_one, gain_two = norm_gains[0, 0], norm_gains[0, 1]
    stream = lax.dynamic_slice_in_dim(tokens, c * size, size, 0).astype(f32)
    cot = lax.dynamic_slice_in_dim(cotangent, c * size, size, 0)
    hidden_own, normed1, scaled1 = layer_norm(stream, gain_one)
    hidden = share(after(hidden_own.astype(bf16), mixer_rows))
    rest = after(rest, mixer_rows)
    rest_rows = join(deal(lambda m: lax.dynamic_index_in_dim(rest, m, 0, keepdims=False)))
    w_o = whole(rest_rows[:, :VALUE])
    w_d = whole(rest_rows[:, VALUE + units :])
    w_u = whole(rest_rows[:, VALUE : VALUE + units])
    cot_all = share(after(cot, hidden[0]), True)

    qkv = [dot(h, w_mixer_all[:, : 2 * KEY + VALUE]).astype(bf16) for h in hidden]
    end_state = state_sum(
        [v[:, KEY : 2 * KEY] for v in qkv], to_end, [v[:, 2 * KEY :] for v in qkv]
    )
    chunk_flops = 2 * size * size * (KEY + VALUE) + 4 * size * KEY * VALUE
    state_in = passed(end_state, 1)
    normed, scale, states = walk(
        forward_kernel,
        cores,
        team,
        edges,
        [qkv],
        [
            (seg_col, (size, 1), True),
            (seg_row, (1, 1, size), True),
            (state_in, (KEY, VALUE), False),
        ],
        [
            (jax.ShapeDtypeStruct((chunks * size, VALUE), f32), (size, VALUE), True),
            (jax.ShapeDtypeStruct((chunks * size, 1), f32), (size, 1), True),
            (jax.ShapeDtypeStruct((chunks, KEY, VALUE), bf16), (1, KEY, VALUE), True),
        ],
        False,
        chunks * chunk_flops,
        chunks * size * 4096,
    )
    gate = [dot(h, w_mixer_all[:, 2 * KEY + VALUE :]) for h in hidden]
    gate = after(gate, state_in)
    gated = []
    for e in near:
        gated.append(
            (gate[e] * jax.nn.sigmoid(gate[e]) * here(normed, e)).astype(bf16)
        )
    half = size // 2
    both = range(2)

    def of_half(value, h):
        return value[h * half : (h + 1) * half]

    gated_half = [
        [v.reshape(team, 2, half, VALUE)[:, h].reshape(-1, VALUE) for h in both] for v in gated
    ]
    grad_act = [dot(t, w_d) for t in cot_all]
    own = None
    streams, normed2, scaled2, hidden2, act, grad_up = [], [], [], [], [], []
    for h in both:
        added = reduce_half(gated, half, h, w_o, 0, own)[0]
        streams.append(of_half(stream, h) + added)
        own, n, s = layer_norm(streams[h], gain_two)
        normed2.append(n)
        scaled2.append(s)
        own = own.astype(bf16)
        hidden2.append(share(own))
        pairs = []
        for e in near:
            pairs.append(unit_step(hidden2[h][e], w_u, grad_act[e], units, h))
        act.append([p[0] for p in pairs])
        grad_up.append([p[1] for p in pairs])

    def both_cores(rows):
        rows = rows.astype(bf16)
        got = [rows] + [swap(rows, "h", e) for e in range(1, cores)]
        return join(straight(got, "h"))

    grad, grad_all, gain_grad_two = [], [], 0.0
    for h in both:
        value, sent = reduce_half(grad_up[h], half, h, w_u, 0, own)
        norm_part, gain_part = norm_back(value, normed2[h], scaled2[h], gain_two)
        gain_grad_two = gain_grad_two + gain_part
        grad.append(of_half(cot, h).astype(f32) + norm_part)
        own = grad[h].astype(bf16)
        grad_all.append(share(own, relay=True))
    cot_late, hidden_late = after((cot_all, hidden2), sent)
    halves = [(e, h) for e in near for h in both]
    part = team * half
    units_done = grads(
        [
            [(hidden_late[h][e], 0, grad_up[h][e], 0) for e, h in halves],
            [(cot_late[e], h, act[h][e], 0) for e, h in halves],
        ],
        part,
        units,
    )
    backs = []
    for e in near:
        grad_here = [grad_all[h][e] for h in both]
        backs.append(gate_back(grad_here, w_o, gate[e], normed, scale, e, team))
    grad_gate, grad_mixed, mixed_rest = ([v[i] for v in backs] for i in range(3))
    heads_done = grads(
        [
            [(grad_all[h][e], 0, gated_half[e][h], 0) for e, h in halves],
            [(hidden[e], h, grad_gate[e], h) for e, h in halves],
        ],
        part,
        VALUE,
    )
    grad_before = state_sum([v[:, :KEY] for v in qkv], from_start, grad_mixed)
    grad_in = passed(grad_before, -1)
    act_rows = [jnp.concatenate([act[h][e] for h in both], axis=0) for e in near]
    added = reduce(after(act_rows, grad_before), w_d, 0, halves=2)[0]
    (proj,) = walk(
        backward_kernel,
        cores,
        team,
        edges,
        [qkv, grad_mixed, mixed_rest, grad_gate],
        [
            (states, (1, KEY, VALUE), True),
            (seg_col, (size, 1), True),
            (seg_row, (1, 1, size), True),
            (grad_in, (KEY, VALUE), False),
        ],
        [
            (
                jax.ShapeDtypeStruct((chunks * size, 2 * KEY + 2 * VALUE), bf16),
                (size, 2 * KEY + 2 * VALUE),
                True,
            ),
        ],
        True,
        3 * chunks * chunk_flops,
        chunks * size * 12000,
    )
    grad_proj = [here(proj, e) for e in near]
    qkv_done = grads([[(hidden[e], 0, proj, e) for e in near]], rows, 2 * KEY + VALUE)
    grad_hidden = reduce(grad_proj, w_mixer_all, 0, proj)[0]
    output = both_cores(jnp.concatenate(streams, axis=0) + added)
    norm_part, gain_grad_one = norm_back(grad_hidden, normed1, scaled1, gain_one)
    input_grad = both_cores(jnp.concatenate(grad, axis=0) + norm_part)
    gain_grad = total(jnp.stack([gain_grad_one, gain_grad_two]))

    def own_rows(done):
        return deal(lambda m: lax.dynamic_slice_in_dim(done, m * rows_here, rows_here, 0))

    own_units = own_rows(units_done)
    own_heads = own_rows(heads_done)
    own_heads = after(own_heads, gain_grad_one)
    own_qkv = own_rows(qkv_done)
    mixer_grad = jnp.concatenate(
        [
            jnp.stack(own_qkv, axis=1),
            jnp.stack([v[:, VALUE:] for v in own_heads], axis=1),
        ],
        axis=-1,
    ).astype(f32)
    up_grad = jnp.concatenate([v[:, :units] for v in own_units], axis=1).astype(f32)
    down_grad = jnp.concatenate([v[:, units:].T for v in own_units], axis=0).astype(f32)
    out_grad = jnp.concatenate([v[:, :VALUE].T for v in own_heads], axis=0).astype(f32)
    return (
        output,
        input_grad,
        gain_grad[None],
        mixer_grad[None],
        out_grad[None],
        up_grad[None],
        down_grad[None],
    )


def solution(mesh):
    devices, cores = mesh.devices.shape
    team = team_size(devices, HEADS // cores)
    fine = Mesh(mesh.devices.reshape(devices // team, team, cores), ("g", "t", "h"))
    fsdp = ("g", "t")

    return jax.shard_map(
        shards,
        mesh=fine,
        in_specs=(
            P(fsdp, None),
            P(),
            P(None, fsdp, "h", None),
            P(None, "h", fsdp),
            P(None, fsdp, "h"),
            P(None, "h", fsdp),
            P(fsdp),
            P(fsdp, None),
        ),
        out_specs=(
            P(fsdp, None),
            P(fsdp, None),
            P(),
            P(None, fsdp, "h", None),
            P(None, "h", fsdp),
            P(None, fsdp, "h"),
            P(None, "h", fsdp),
        ),
        check_vma=False,
    )
```
